32 devices in a mesh: wide: 4 (over z), grp: 4 (over y, x), rep: 2 (over core).
Axes of the slice: x: 2, y: 2, z: 4, core: 2. Of those that a mesh axis runs over, the one named last changes fastest.
Arguments:
- hidden_in: bfloat16 [1024, 2048], P(('wide', 'rep'), 'grp'), may hold values from -6 to 6
- grad_out: bfloat16 [1024, 2048], P(('wide', 'rep'), 'grp'), may hold values from -6 to 6
- route_ids: int32 [1024, 8], P(('wide', 'rep')), may hold values from 0 to 15, all different within a row; in each aligned block of 128 rows (0 to 127, 128 to 255, ...) at most 96 rows name the same one
- route_weights: float32 [1024, 8], P(('wide', 'rep')), may hold values from 0.05 to 1
- gate_proj: bfloat16 [16, 2048, 768], P('wide', None, 'rep'), may hold values from -0.125 to 0.125
- up_proj: bfloat16 [16, 2048, 768], P('wide', None, 'rep'), may hold values from -0.125 to 0.125
- down_proj: bfloat16 [16, 768, 2048], P('wide', 'rep'), may hold values from -0.21875 to 0.21875
Outputs:
- grad_in: bfloat16 [1024, 2048], P(('wide', 'rep'), 'grp')
The draws below stay inside these ranges and needn't reach their ends.
Inputs may be any that keep to these rules, and one draw needn't show every extreme that they name: `route_ids`: each row names 8 different experts. In each aligned block of 128 rows (the rows of one index of wide+rep) no expert is named by more than 96 rows, a bound that some block reaches.
All inputs are finite; a program needn't handle non-finite values.
Results may differ from the reference program's by a relative error of at most 0.0064.
Values may be sent and summed in bfloat16 or wider, within the bound.
No kernel may reach another device: no remote copies, remote signals or barrier semaphores. Data moves between devices by JAX's collectives and lax.ppermute only.
A program may use at most 128 MiB of HBM per device.

```python
import math
import jax
import jax.numpy as jnp
import numpy as np
from jax import lax

D = 2048
FF = 768
TOP = 8
TOK_DEV = 128
EXPERTS = 16
CAP = 96
TOKENS = 1024


def steps_of(stream_key, extent, split, smallest, largest):
    gain = 1.0
    for position, shards_of in split:
        heights = jax.random.uniform(jax.random.fold_in(jax.random.fold_in(stream_key, 6), position), (shards_of,), jnp.float32, smallest / len(split), largest / len(split))
        gain = gain * jnp.repeat(jnp.exp(heights), extent[position] // shards_of).reshape((-1,) + (1,) * (len(extent) - 1 - position))
    return gain


def assign_block(rng, own, number, rows, count, top, bound, skew):
    order = jax.random.permutation(rng, count)
    heavy_load, ordinary = shares(count, rows * top, bound, skew, True), shares(count, rows * top, bound, skew, False)
    places = jnp.arange(count)

    def named(tallies, offset_by):
        used = int((tallies > 0).sum())
        fixed = max(1, used // 4)
        shifted = fixed + (places - fixed + offset_by * (used - fixed)) % max(1, count - fixed)
        return jnp.zeros((count,), jnp.int32).at[order[jnp.where(places < fixed, places, shifted)]].set(jnp.asarray(tallies, jnp.int32))

    tallies = jnp.where(number % 4 == 0, named(heavy_load, number // 4), named(ordinary, number - number // 4 - 1))
    mixed = jax.random.permutation(jax.random.fold_in(own, 3), count)
    source_of, taker = mixed[0:count // 2 * 2:2], mixed[1:count // 2 * 2:2]
    slack = jnp.minimum(tallies[source_of] - 1, bound - tallies[taker]) // 2
    slack = jnp.where((source_of == order[0]) | (taker == order[0]) | (tallies[taker] == 0), 0, jnp.maximum(slack, 0))
    shifted = jax.random.randint(jax.random.fold_in(own, 4), (count // 2,), 0, 1 << 20) % (slack + 1)
    tallies = tallies.at[source_of].add(-shifted).at[taker].add(shifted)
    members = jnp.searchsorted(jnp.cumsum(tallies), jnp.arange(rows * top), side="right").astype(jnp.int32)
    listing = members.reshape(top, rows).T
    listing = listing[jax.random.permutation(jax.random.fold_in(own, 1), rows)]
    offset_by = jax.random.randint(jax.random.fold_in(own, 2), (rows, 1), 0, top)
    return jnp.take_along_axis(listing, (jnp.arange(top)[None, :] + offset_by) % top, axis=1)


def shares(number_of, total, reach, lean, full):
    portions = [(1 << 20) // math.isqrt(grade ** lean) + 1 for grade in range(1, number_of + 1)]
    largest = reach if full else min(reach, max(-(-total // number_of), total * portions[0] // sum(portions)))
    least = 1 if total - largest >= number_of - 1 else 0
    given, rest = [largest] + [least] * (number_of - 1), total - largest - least * (number_of - 1)
    while rest > 0:
        candidates = [i for i in range(1, number_of) if given[i] < largest] or [i for i in range(1, number_of) if given[i] < reach]
        whole, remaining = sum([portions[i] for i in candidates]), rest
        for i in candidates:
            addition = min(reach - given[i], max(1, remaining * portions[i] // whole), rest)
            given[i] = given[i] + addition
            rest = rest - addition
    return np.array(given)


def noise(stream_key, dims, scale, reach, cuts=(), kind=jnp.bfloat16):
    values = scale * jax.random.normal(stream_key, dims, jnp.float32)
    if cuts:
        values = values * steps_of(stream_key, dims, cuts, -0.22, 0.18)
    return jnp.clip(values, -reach, reach).astype(kind)


def setup_inputs(seed: int = 0) -> dict:
    arg_keys = jax.random.split(jax.random.key(seed), 8)
    hidden_in = noise(arg_keys[0], (TOKENS, D), 1.0, 6.0, ((0, 8), (1, 4)))
    grad_out = noise(arg_keys[1], (TOKENS, D), 1.0, 6.0, ((0, 8), (1, 4)))
    route_ids_keys = jax.random.split(jax.random.fold_in(arg_keys[2], 1), TOKENS // TOK_DEV)
    route_ids_turns = jax.random.permutation(jax.random.fold_in(arg_keys[2], 3), TOKENS // TOK_DEV)
    route_ids = jax.vmap(lambda own, number: assign_block(jax.random.fold_in(arg_keys[2], 2), own, number, TOK_DEV, EXPERTS, TOP, CAP, 2))(route_ids_keys, route_ids_turns).reshape((TOKENS, TOP))
    route_weights = jnp.clip(0.05 + 0.95 * jax.random.uniform(arg_keys[3], (TOKENS, TOP), jnp.float32) ** steps_of(arg_keys[3], (TOKENS, TOP), ((0, 8),), -0.2, 0.2), 0.05, 1.0)
    gate_proj = noise(arg_keys[4], (EXPERTS, D, FF), D ** -0.5, 0.125, ((0, 4), (2, 2)))
    up_proj = noise(arg_keys[5], (EXPERTS, D, FF), D ** -0.5, 0.125, ((0, 4), (2, 2)))
    down_proj = noise(arg_keys[6], (EXPERTS, FF, D), FF ** -0.5, 0.21875, ((0, 4), (1, 2)))
    return {"hidden_in": hidden_in, "grad_out": grad_out, "route_ids": route_ids, "route_weights": route_weights, "gate_proj": gate_proj, "up_proj": up_proj, "down_proj": down_proj}


def expert_grad(inputs, scaled, gate_mat, up_mat, down_mat):
    pre_gate = jnp.dot(inputs, gate_mat, preferred_element_type=jnp.float32)
    pre_up = jnp.dot(inputs, up_mat, preferred_element_type=jnp.float32)
    back_hidden = jnp.dot(scaled, down_mat.T, preferred_element_type=jnp.float32)
    gate_sig = jax.nn.sigmoid(pre_gate)
    d_gate = (back_hidden * pre_up * gate_sig * (1.0 + pre_gate * (1.0 - gate_sig))).astype(jnp.bfloat16)
    d_up = (back_hidden * pre_gate * gate_sig).astype(jnp.bfloat16)
    summed = jnp.dot(d_gate, gate_mat.T, preferred_element_type=jnp.float32) + jnp.dot(d_up, up_mat.T, preferred_element_type=jnp.float32)
    return summed.astype(jnp.bfloat16)

def reference(hidden_in, grad_out, route_ids, route_weights, gate_proj, up_proj, down_proj):
    blocks = TOKENS // TOK_DEV
    per_block = TOK_DEV * TOP
    route_block = route_ids.reshape(blocks, per_block).astype(jnp.int32)
    onehot = (route_block[:, :, None] == jnp.arange(EXPERTS, dtype=jnp.int32)[None, None, :]).astype(jnp.int32)
    slot_rank = lax.optimization_barrier(jnp.sum((jnp.cumsum(onehot, axis=1) - onehot) * onehot, axis=2)).astype(jnp.int32)
    block_ids = jnp.arange(blocks, dtype=jnp.int32)[:, None]
    column = block_ids * CAP + slot_rank
    token_ids = block_ids * TOK_DEV + jnp.arange(per_block, dtype=jnp.int32)[None, :] // TOP
    table_tok = jnp.full((EXPERTS, blocks * CAP), TOKENS, jnp.int32).at[route_block, column].set(token_ids)
    table_wt = jnp.zeros((EXPERTS, blocks * CAP), jnp.float32).at[route_block, column].set(route_weights.reshape(blocks, per_block))
    padded_in = jnp.concatenate([hidden_in, jnp.zeros((1, D), hidden_in.dtype)], axis=0)
    padded_out = jnp.concatenate([grad_out, jnp.zeros((1, D), grad_out.dtype)], axis=0)

    def one_expert(running, expert):
        tok_index = table_tok[expert]
        inputs = padded_in[tok_index]
        scaled = (table_wt[expert][:, None] * padded_out[tok_index].astype(jnp.float32)).astype(jnp.bfloat16)
        pair_grad = expert_grad(inputs, scaled, gate_proj[expert], up_proj[expert], down_proj[expert])
        return (running.at[tok_index].add(pair_grad.astype(jnp.float32)), None)
    accum_grad, unused = lax.scan(one_expert, jnp.zeros((TOKENS + 1, D), jnp.float32), jnp.arange(EXPERTS, dtype=jnp.int32))
    return accum_grad[:TOKENS].astype(jnp.bfloat16)
```

```python
import jax
import jax.numpy as jnp
from jax import lax
from jax.experimental import pallas as pl
from jax.experimental.pallas import tpu as pltpu
from jax.sharding import PartitionSpec as P


def expert_back(stacked, gate_mat, up_mat, down_mat):
    inputs = stacked[0]
    scaled = stacked[1]
    pre_gate = jnp.einsum("wecd,edf->wecf", inputs, gate_mat, preferred_element_type=jnp.float32)
    pre_up = jnp.einsum("wecd,edf->wecf", inputs, up_mat, preferred_element_type=jnp.float32)
    back_hidden = jnp.einsum("wecd,efd->wecf", scaled, down_mat, preferred_element_type=jnp.float32)
    gate_sig = jax.nn.sigmoid(pre_gate)
    d_gate = (back_hidden * pre_up * gate_sig * (1.0 + pre_gate * (1.0 - gate_sig))).astype(
        jnp.bfloat16
    )
    d_up = (back_hidden * pre_gate * gate_sig).astype(jnp.bfloat16)
    first_term = jnp.einsum("wecf,edf->wecd", d_gate, gate_mat, preferred_element_type=jnp.float32)
    return first_term + jnp.einsum(
        "wecf,edf->wecd", d_up, up_mat, preferred_element_type=jnp.float32
    )


def slot_ranks(pair_ids, experts):
    pairs = pair_ids.shape[0]
    block = 128
    nblocks = pairs // block
    onehot = (pair_ids[:, None] == jnp.arange(experts, dtype=jnp.int32)[None, :]).astype(
        jnp.bfloat16
    )
    onehot = onehot.reshape(nblocks, block, experts)
    lower = (
        lax.broadcasted_iota(jnp.int32, (block, block), 0)
        > lax.broadcasted_iota(jnp.int32, (block, block), 1)
    ).astype(jnp.bfloat16)
    within = jnp.einsum("ij,bje->bie", lower, onehot, preferred_element_type=jnp.float32)
    totals = jnp.sum(onehot.astype(jnp.float32), axis=1)
    before = jnp.cumsum(totals, axis=0) - totals
    counted = jnp.sum((within + before[:, None, :]) * onehot.astype(jnp.float32), axis=2)
    return counted.reshape(pairs).astype(jnp.int32)


def routed_shards(hidden_in, grad_out, route_ids, route_weights, gate_proj, up_proj, down_proj):
    tok_rows, local_cols = hidden_in.shape
    fanout = route_ids.shape[1]
    wide_size = lax.axis_size("wide")
    groups = lax.axis_size("grp")
    local_experts = gate_proj.shape[0]
    experts = local_experts * wide_size
    capacity = groups * max(1, 3 * tok_rows * fanout // (2 * experts * groups))
    pair_ids = route_ids.reshape(-1)
    slot_rank = slot_ranks(pair_ids, experts)
    position = pair_ids * capacity + slot_rank
    token_ids = jnp.arange(tok_rows * fanout, dtype=jnp.int32) // fanout
    pair_inputs = hidden_in[token_ids]
    pair_scaled = (
        route_weights.reshape(-1)[:, None] * grad_out[token_ids].astype(jnp.float32)
    ).astype(jnp.bfloat16)
    blank_rows = jnp.zeros((experts * capacity, local_cols), jnp.bfloat16)
    outgoing = jnp.stack(
        [blank_rows.at[position].set(pair_inputs), blank_rows.at[position].set(pair_scaled)]
    )
    outgoing = outgoing.reshape(2, wide_size, local_experts, capacity, local_cols)
    received = lax.all_to_all(
        lax.all_to_all(outgoing, "wide", split_axis=1, concat_axis=1, tiled=True),
        "grp",
        split_axis=3,
        concat_axis=4,
        tiled=True,
    )
    full_gate, full_up, full_down = (
        lax.all_gather(gate_proj, "rep", axis=2, tiled=True),
        lax.all_gather(up_proj, "rep", axis=2, tiled=True),
        lax.all_gather(down_proj, "rep", axis=1, tiled=True),
    )
    summed = expert_back(received, full_gate, full_up, full_down)
    returned = lax.all_to_all(
        lax.all_to_all(
            summed.astype(jnp.bfloat16), "wide", split_axis=0, concat_axis=0, tiled=True
        ),
        "grp",
        split_axis=3,
        concat_axis=2,
        tiled=True,
    )
    flat_rows = returned.reshape(experts * capacity, local_cols)
    picked = flat_rows[position].astype(jnp.float32).reshape(tok_rows, fanout, local_cols)
    return jnp.sum(picked, axis=1).astype(jnp.bfloat16)


LANES = 128
CONTRACT_LAST = (((1,), (1,)), ((), ()))


def fill_rows(place, blocks, rows_buf, groups):
    height = blocks[0].shape[0]
    cols = rows_buf.shape[1] // groups
    for number, block in enumerate(blocks):
        for step in range(groups):
            start = pl.multiple_of((place ^ step) * cols, LANES)
            rows_buf[number * height : (number + 1) * height, pl.ds(start, cols)] = block[
                :, step * cols : (step + 1) * cols
            ]


def weight_copies(gate_hbm, up_hbm, both, sems):
    half = gate_hbm.shape[2]
    copies = []
    for e in range(gate_hbm.shape[0]):
        copies.append(
            (
                pltpu.make_async_copy(gate_hbm.at[e], both.at[e, :, :half], sems.at[e, 0]),
                pltpu.make_async_copy(up_hbm.at[e], both.at[e, :, half:], sems.at[e, 1]),
            )
        )
    return copies


def pre_kernel(groups, count, *refs):
    place = refs[0][0]
    blocks = refs[1 : 1 + count]
    gate_hbm, up_hbm, pre_out, both, rows_buf, sems = refs[1 + count :]
    copies = weight_copies(gate_hbm, up_hbm, both, sems)
    for pair in copies:
        for copy in pair:
            copy.start()
    fill_rows(place, blocks, rows_buf, groups)
    for e, pair in enumerate(copies):
        for copy in pair:
            copy.wait()
        pre_out[e] = jnp.dot(rows_buf[...], both[e], preferred_element_type=jnp.float32)


def pre_activations(place, blocks, gate_proj, up_proj, groups):
    local, width, half = gate_proj.shape
    rows = len(blocks) * blocks[0].shape[0]
    vmem = pl.BlockSpec(memory_space=pltpu.VMEM)
    return pl.pallas_call(
        lambda *refs: pre_kernel(groups, len(blocks), *refs),
        in_specs=[pl.BlockSpec(memory_space=pltpu.SMEM)]
        + [vmem] * len(blocks)
        + [pl.BlockSpec(memory_space=pl.ANY)] * 2,
        out_specs=vmem,
        out_shape=jax.ShapeDtypeStruct((local, rows, 2 * half), jnp.float32),
        scratch_shapes=[
            pltpu.VMEM((local, width, 2 * half), jnp.bfloat16),
            pltpu.VMEM((rows, width), jnp.bfloat16),
            pltpu.SemaphoreType.DMA((local, 2)),
        ],
        compiler_params=pltpu.CompilerParams(vmem_limit_bytes=24 << 20),
        cost_estimate=pl.CostEstimate(
            flops=4 * rows * width * half * local,
            bytes_accessed=4 * local * width * half,
            transcendentals=0,
        ),
        name="pre",
    )(place, *blocks, gate_proj, up_proj)


def post_kernel(groups, count, *refs):
    place = refs[0][0]
    blocks = refs[1 : 1 + count]
    pre_ref, gate_hbm, up_hbm, down_hbm = refs[1 + count : 5 + count]
    mine_out, other_out, both, down, rows_buf, total, sems, down_sems = refs[5 + count :]
    local, width, double = both.shape
    half = double // 2
    height = blocks[0].shape[0]
    copies = weight_copies(gate_hbm, up_hbm, both, sems)
    down_copies = [
        pltpu.make_async_copy(down_hbm.at[e], down.at[pl.ds(e * half, half), :], down_sems.at[e])
        for e in range(local)
    ]
    for e in range(local):
        down_copies[e].start()
        for copy in copies[e]:
            copy.start()
    fill_rows(place, blocks, rows_buf, groups)
    weights = jnp.concatenate([block[:, width : width + LANES] for block in blocks], axis=0)
    weights = weights.astype(jnp.float32)
    lane = lax.broadcasted_iota(jnp.int32, weights.shape, 1)
    first = refs[0][1] * local
    experts = local * (count // 2)
    for e in range(local):
        down_copies[e].wait()
        named = (lane == first + e) | (lane == first + e + experts)
        route = jnp.sum(jnp.where(named, weights, 0.0), axis=1, keepdims=True)
        back = route * lax.dot_general(
            rows_buf[...],
            down[e * half : (e + 1) * half],
            CONTRACT_LAST,
            preferred_element_type=jnp.float32,
        )
        pre_gate = pre_ref[e, :, :half]
        pre_up = pre_ref[e, :, half:]
        sig = 1.0 / (1.0 + jnp.exp(-pre_gate))
        d_gate = back * pre_up * sig * (1.0 + pre_gate * (1.0 - sig))
        d_up = back * pre_gate * sig
        hidden = jnp.concatenate([d_gate, d_up], axis=1).astype(jnp.bfloat16)
        for copy in copies[e]:
            copy.wait()
        term = lax.dot_general(hidden, both[e], CONTRACT_LAST, preferred_element_type=jnp.float32)
        if e == 0:
            total[...] = term
        else:
            total[...] += term
    cols = width // groups
    for number in range(count):
        target = mine_out if number < count // 2 else other_out
        for step in range(groups):
            start = pl.multiple_of((place ^ step) * cols, LANES)
            target[number % (count // 2), :, step * cols : (step + 1) * cols] = total[
                number * height : (number + 1) * height, pl.ds(start, cols)
            ].astype(jnp.bfloat16)


def input_gradient(place, blocks, pre_act, gate_proj, up_proj, down_proj, groups):
    local, width, half = gate_proj.shape
    count, height = len(blocks), blocks[0].shape[0]
    rows = count * height
    vmem = pl.BlockSpec(memory_space=pltpu.VMEM)
    part = jax.ShapeDtypeStruct((count // 2, height, width), jnp.bfloat16)
    return pl.pallas_call(
        lambda *refs: post_kernel(groups, count, *refs),
        in_specs=[pl.BlockSpec(memory_space=pltpu.SMEM)]
        + [vmem] * (count + 1)
        + [pl.BlockSpec(memory_space=pl.ANY)] * 3,
        out_specs=[vmem, vmem],
        out_shape=[part, part],
        scratch_shapes=[
            pltpu.VMEM((local, width, 2 * half), jnp.bfloat16),
            pltpu.VMEM((local * half, width), jnp.bfloat16),
            pltpu.VMEM((rows, width), jnp.bfloat16),
            pltpu.VMEM((rows, width), jnp.float32),
            pltpu.SemaphoreType.DMA((local, 2)),
            pltpu.SemaphoreType.DMA((local,)),
        ],
        compiler_params=pltpu.CompilerParams(vmem_limit_bytes=40 << 20),
        cost_estimate=pl.CostEstimate(
            flops=6 * rows * width * half * local,
            bytes_accessed=6 * local * width * half,
            transcendentals=rows * half * local,
        ),
        name="post",
    )(place, *blocks, pre_act, gate_proj, up_proj, down_proj)


def flip(array, axis, step):
    size = lax.axis_size(axis)
    return lax.ppermute(array, axis, [(i, i ^ step) for i in range(size)])


def route_table(route_ids, route_weights, experts):
    chosen = route_ids[:, :, None] == jnp.arange(experts, dtype=jnp.int32)[None, None, :]
    return jnp.sum(jnp.where(chosen, route_weights[:, :, None], 0.0), axis=1)


def gathered(block, axis):
    size = lax.axis_size(axis)
    parts = {0: block}
    step = size // 2
    while step:
        for k in sorted(parts):
            parts[k | step] = flip(parts[k], axis, step)
        step //= 2
    return [parts[k] for k in range(size)]


def dense_shards(hidden_in, grad_out, route_ids, route_weights, gate_proj, up_proj, down_proj):
    tok_rows, cols = hidden_in.shape
    wide_size = lax.axis_size("wide")
    groups = lax.axis_size("grp")
    local = gate_proj.shape[0]
    height = tok_rows // groups
    place = lax.axis_index("grp")
    place_array = place.reshape(1).astype(jnp.int32)
    wide = lax.axis_index("wide")

    def slices_of(array):
        pieces = []
        for step in range(groups):
            piece = lax.dynamic_slice_in_dim(array, (place ^ step) * height, height, 0)
            pieces.append(piece if step == 0 else flip(piece, "grp", step))
        return pieces

    hidden_pieces = slices_of(hidden_in)
    table = route_table(route_ids, route_weights, local * wide_size)
    table = lax.dynamic_slice_in_dim(table, place * height, height, 0)
    high = table.astype(jnp.bfloat16)
    low = (table - high.astype(jnp.float32)).astype(jnp.bfloat16)
    packed = jnp.concatenate([high, low], axis=1)
    packed = jnp.pad(packed, ((0, 0), (0, LANES - packed.shape[1])))
    hidden_block = jnp.concatenate(hidden_pieces, axis=1)
    grad_block = jnp.concatenate(slices_of(grad_out) + [packed], axis=1)
    hidden_blocks = gathered(hidden_block, "wide")
    grad_blocks = gathered(grad_block, "wide")
    hidden_all = hidden_blocks + [flip(b, "rep", 1) for b in hidden_blocks]
    grad_all = grad_blocks + [flip(b, "rep", 1) for b in grad_blocks]
    pre_act = pre_activations(place_array, hidden_all, gate_proj, up_proj, groups)
    scalars = jnp.stack([place.astype(jnp.int32), wide.astype(jnp.int32)])
    mine, other = input_gradient(scalars, grad_all, pre_act, gate_proj, up_proj, down_proj, groups)
    swapped = flip(other, "rep", 1)
    partial = (mine.astype(jnp.float32) + swapped.astype(jnp.float32)).astype(jnp.bfloat16)
    returned = [flip(partial[k], "wide", k) for k in range(1, wide_size)]
    summed = partial[0].astype(jnp.float32)
    for part in returned:
        summed = summed + part.astype(jnp.float32)
    summed = summed.astype(jnp.bfloat16)
    pieces = []
    for step in range(groups):
        piece = summed[:, step * cols : (step + 1) * cols]
        pieces.append(piece if step == 0 else flip(piece, "grp", step))
    bit = 1
    while bit < groups:
        swap = (place & bit) != 0
        pieces = [jnp.where(swap, pieces[k ^ bit], pieces[k]) for k in range(groups)]
        bit *= 2
    return jnp.concatenate(pieces, axis=0)


def shards(hidden_in, grad_out, route_ids, route_weights, gate_proj, up_proj, down_proj):
    wide_size, groups = lax.axis_size("wide"), lax.axis_size("grp")
    experts = gate_proj.shape[0] * wide_size
    fanout = route_ids.shape[1]
    powers = all(n & (n - 1) == 0 for n in (wide_size, groups))
    dense = powers and experts <= 2 * fanout and 2 * experts <= LANES and lax.axis_size("rep") == 2
    path = dense_shards if dense else routed_shards
    return path(
        hidden_in, grad_out, route_ids, route_weights, gate_proj, up_proj, down_proj
    )


def solution(mesh):
    in_specs = (
        P(("wide", "rep"), "grp"),
        P(("wide", "rep"), "grp"),
        P(("wide", "rep"), None),
        P(("wide", "rep"), None),
        P("wide", None, "rep"),
        P("wide", None, "rep"),
        P("wide", "rep", None),
    )
    out_specs = P(("wide", "rep"), "grp")
    return jax.shard_map(shards, mesh=mesh, in_specs=in_specs, out_specs=out_specs, check_vma=False)
```

```python
import jax
import jax.numpy as jnp
from jax import lax
from jax.experimental import pallas as pl
from jax.experimental.pallas import tpu as pltpu
from jax.sharding import PartitionSpec as P


def expert_back(stacked, gate_mat, up_mat, down_mat):
    inputs = stacked[0]
    scaled = stacked[1]
    pre_gate = jnp.einsum("wecd,edf->wecf", inputs, gate_mat, preferred_element_type=jnp.float32)
    pre_up = jnp.einsum("wecd,edf->wecf", inputs, up_mat, preferred_element_type=jnp.float32)
    back_hidden = jnp.einsum("wecd,efd->wecf", scaled, down_mat, preferred_element_type=jnp.float32)
    gate_sig = jax.nn.sigmoid(pre_gate)
    d_gate = (back_hidden * pre_up * gate_sig * (1.0 + pre_gate * (1.0 - gate_sig))).astype(
        jnp.bfloat16
    )
    d_up = (back_hidden * pre_gate * gate_sig).astype(jnp.bfloat16)
    first_term = jnp.einsum("wecf,edf->wecd", d_gate, gate_mat, preferred_element_type=jnp.float32)
    return first_term + jnp.einsum(
        "wecf,edf->wecd", d_up, up_mat, preferred_element_type=jnp.float32
    )


def slot_ranks(pair_ids, experts):
    pairs = pair_ids.shape[0]
    block = 128
    nblocks = pairs // block
    onehot = (pair_ids[:, None] == jnp.arange(experts, dtype=jnp.int32)[None, :]).astype(
        jnp.bfloat16
    )
    onehot = onehot.reshape(nblocks, block, experts)
    lower = (
        lax.broadcasted_iota(jnp.int32, (block, block), 0)
        > lax.broadcasted_iota(jnp.int32, (block, block), 1)
    ).astype(jnp.bfloat16)
    within = jnp.einsum("ij,bje->bie", lower, onehot, preferred_element_type=jnp.float32)
    totals = jnp.sum(onehot.astype(jnp.float32), axis=1)
    before = jnp.cumsum(totals, axis=0) - totals
    counted = jnp.sum((within + before[:, None, :]) * onehot.astype(jnp.float32), axis=2)
    return counted.reshape(pairs).astype(jnp.int32)


def routed_shards(hidden_in, grad_out, route_ids, route_weights, gate_proj, up_proj, down_proj):
    tok_rows, local_cols = hidden_in.shape
    fanout = route_ids.shape[1]
    wide_size = lax.axis_size("wide")
    groups = lax.axis_size("grp")
    local_experts = gate_proj.shape[0]
    experts = local_experts * wide_size
    capacity = groups * max(1, 3 * tok_rows * fanout // (2 * experts * groups))
    pair_ids = route_ids.reshape(-1)
    slot_rank = slot_ranks(pair_ids, experts)
    position = pair_ids * capacity + slot_rank
    token_ids = jnp.arange(tok_rows * fanout, dtype=jnp.int32) // fanout
    pair_inputs = hidden_in[token_ids]
    pair_scaled = (
        route_weights.reshape(-1)[:, None] * grad_out[token_ids].astype(jnp.float32)
    ).astype(jnp.bfloat16)
    blank_rows = jnp.zeros((experts * capacity, local_cols), jnp.bfloat16)
    outgoing = jnp.stack(
        [blank_rows.at[position].set(pair_inputs), blank_rows.at[position].set(pair_scaled)]
    )
    outgoing = outgoing.reshape(2, wide_size, local_experts, capacity, local_cols)
    received = lax.all_to_all(
        lax.all_to_all(outgoing, "wide", split_axis=1, concat_axis=1, tiled=True),
        "grp",
        split_axis=3,
        concat_axis=4,
        tiled=True,
    )
    full_gate, full_up, full_down = (
        lax.all_gather(gate_proj, "rep", axis=2, tiled=True),
        lax.all_gather(up_proj, "rep", axis=2, tiled=True),
        lax.all_gather(down_proj, "rep", axis=1, tiled=True),
    )
    summed = expert_back(received, full_gate, full_up, full_down)
    returned = lax.all_to_all(
        lax.all_to_all(
            summed.astype(jnp.bfloat16), "wide", split_axis=0, concat_axis=0, tiled=True
        ),
        "grp",
        split_axis=3,
        concat_axis=2,
        tiled=True,
    )
    flat_rows = returned.reshape(experts * capacity, local_cols)
    picked = flat_rows[position].astype(jnp.float32).reshape(tok_rows, fanout, local_cols)
    return jnp.sum(picked, axis=1).astype(jnp.bfloat16)


LANES = 128
VMEM = pl.BlockSpec(memory_space=pltpu.VMEM)
SMEM = pl.BlockSpec(memory_space=pltpu.SMEM)
HBM = pl.BlockSpec(memory_space=pltpu.HBM)


def load_kernel(gate_hbm, up_hbm, down_hbm, after, scalars, both, both_t, down_t, down, sems):
    local, _, half = gate_hbm.shape
    copies = []
    for e in range(local):
        copies.append(
            (
                pltpu.make_async_copy(gate_hbm.at[e], both.at[e, :, :half], sems.at[e, 0]),
                pltpu.make_async_copy(up_hbm.at[e], both.at[e, :, half:], sems.at[e, 1]),
                pltpu.make_async_copy(down_hbm.at[e], down.at[e], sems.at[e, 2]),
            )
        )
        for copy in copies[e]:
            copy.start()
    for e in range(local):
        for copy in copies[e]:
            copy.wait()
        both_t[e] = both[e].T
        down_t[:, e * half : (e + 1) * half] = down[e].T


def load_weights(gate_proj, up_proj, down_proj, after, scalars):
    local, width, half = gate_proj.shape
    size = 6 * local * width * half
    weights = [pltpu.with_memory_space_constraint(w, pltpu.HBM) for w in (gate_proj, up_proj, down_proj)]
    return pl.pallas_call(
        load_kernel,
        in_specs=[HBM] * 3 + [VMEM, SMEM],
        out_specs=[VMEM] * 3,
        out_shape=[
            jax.ShapeDtypeStruct((local, width, 2 * half), jnp.bfloat16),
            jax.ShapeDtypeStruct((local, 2 * half, width), jnp.bfloat16),
            jax.ShapeDtypeStruct((width, local * half), jnp.bfloat16),
        ],
        scratch_shapes=[
            pltpu.VMEM(down_proj.shape, jnp.bfloat16),
            pltpu.SemaphoreType.DMA((local, 3)),
        ],
        compiler_params=pltpu.CompilerParams(vmem_limit_bytes=8 << 20),
        cost_estimate=pl.CostEstimate(flops=0, bytes_accessed=size, transcendentals=0),
        name="load",
    )(*weights, after, scalars)


def chunk_kernel(groups, count, scalars, *refs):
    place, wide = scalars[0], scalars[1]
    blocks = refs[:count]
    both, both_t, down_t, mine_out, other_out, x_rows, g_rows, total = refs[count:]
    local, width, double = both.shape
    half = double // 2
    height = blocks[0].shape[0]
    cols = width // groups
    for number, block in enumerate(blocks):
        rows = slice(number * height, (number + 1) * height)
        for step in range(groups):
            start = pl.multiple_of((place ^ step) * cols, LANES)
            x_rows[rows, pl.ds(start, cols)] = block[:, 2 * step * cols : (2 * step + 1) * cols]
            g_rows[rows, pl.ds(start, cols)] = block[:, (2 * step + 1) * cols : (2 * step + 2) * cols]
    weights = jnp.concatenate([block[:, 2 * width :] for block in blocks], axis=0)
    weights = weights.astype(jnp.float32)
    lane = lax.broadcasted_iota(jnp.int32, weights.shape, 1)
    experts = weights.shape[1] // 2

    for e in range(local):
        named = (lane == wide * local + e) | (lane == wide * local + e + experts)
        route = jnp.sum(jnp.where(named, weights, 0.0), axis=1, keepdims=True)
        pre = jnp.dot(x_rows[...], both[e], preferred_element_type=jnp.float32)
        if e % 2 == 0:
            paired = min(2, local - e)
            back_pair = jnp.dot(
                g_rows[...],
                down_t[:, e * half : (e + paired) * half],
                preferred_element_type=jnp.float32,
            )
        back = route * back_pair[:, (e % 2) * half : (e % 2 + 1) * half]
        pre_gate, pre_up = pre[:, :half], pre[:, half:]
        sig = 1.0 / (1.0 + jnp.exp(-pre_gate))
        d_gate = back * pre_up * sig * (1.0 + pre_gate * (1.0 - sig))
        d_up = back * pre_gate * sig
        hidden = jnp.concatenate([d_gate, d_up], axis=1).astype(jnp.bfloat16)
        term = jnp.dot(hidden, both_t[e], preferred_element_type=jnp.float32)
        if e == 0:
            total[...] = term
        else:
            total[...] += term
    for number in range(count):
        rows = slice(number * height, (number + 1) * height)
        out = mine_out if number < count // 2 else other_out
        for step in range(groups):
            start = pl.multiple_of((place ^ step) * cols, LANES)
            part = total[rows, pl.ds(start, cols)]
            out[number % (count // 2), :, step * cols : (step + 1) * cols] = part.astype(out.dtype)


def chunk_gradient(scalars, mine, other, weights, groups):
    local, width, double = weights[0].shape
    slots, height = len(mine), mine[0].shape[0]
    rows = 2 * slots * height
    return pl.pallas_call(
        lambda *refs: chunk_kernel(groups, 2 * slots, *refs),
        in_specs=[SMEM] + [VMEM] * (2 * slots + 3),
        out_specs=[VMEM, VMEM],
        out_shape=[
            jax.ShapeDtypeStruct((slots, height, width), jnp.float32),
            jax.ShapeDtypeStruct((slots, height, width), jnp.bfloat16),
        ],
        scratch_shapes=[
            pltpu.VMEM((rows, width), jnp.bfloat16),
            pltpu.VMEM((rows, width), jnp.bfloat16),
            pltpu.VMEM((rows, width), jnp.float32),
        ],
        compiler_params=pltpu.CompilerParams(vmem_limit_bytes=16 * rows * width),
        cost_estimate=pl.CostEstimate(
            flops=10 * 256 * width * (double // 2) * local // 2,
            bytes_accessed=4 * rows * width,
            transcendentals=rows * (double // 2) * local,
        ),
        name="chunk",
    )(scalars, *mine, *other, *weights)


def join_kernel(mine, swapped, *outs):
    for number, out in enumerate(outs):
        out[...] = (mine[number] + swapped[number].astype(jnp.float32)).astype(out.dtype)


def join(mine, swapped, kinds):
    shape = mine.shape[1:]
    return pl.pallas_call(
        join_kernel,
        in_specs=[VMEM] * 2,
        out_specs=[VMEM] * len(kinds),
        out_shape=[jax.ShapeDtypeStruct(shape, kind) for kind in kinds],
        compiler_params=pltpu.CompilerParams(vmem_limit_bytes=1 << 20),
        name="join",
    )(mine, swapped)


def flip(array, axis, step):
    size = lax.axis_size(axis)
    return lax.ppermute(array, axis, [(i, i ^ step) for i in range(size)])


def route_table(route_ids, route_weights, experts):
    chosen = route_ids[:, :, None] == jnp.arange(experts, dtype=jnp.int32)[None, None, :]
    return jnp.sum(jnp.where(chosen, route_weights[:, :, None], 0.0), axis=1)


def gathered(block, axis):
    size = lax.axis_size(axis)
    parts = {0: block}
    step = size // 2
    while step:
        for k in sorted(parts):
            parts[k | step] = flip(parts[k], axis, step)
        step //= 2
    return [parts[k] for k in range(size)]


def dense_shards(hidden_in, grad_out, route_ids, route_weights, gate_proj, up_proj, down_proj):
    tok_rows, cols = hidden_in.shape
    wide_size = lax.axis_size("wide")
    groups = lax.axis_size("grp")
    local = gate_proj.shape[0]
    height = tok_rows // groups
    place = lax.axis_index("grp").astype(jnp.int32)
    wide = lax.axis_index("wide").astype(jnp.int32)
    scalars = jnp.stack([place, wide])

    pieces = []
    for step in range(groups):
        first = (place ^ step) * height
        piece = jnp.concatenate(
            [lax.dynamic_slice_in_dim(a, first, height, 0) for a in (hidden_in, grad_out)], axis=1
        )
        pieces.append(piece if step == 0 else flip(piece, "grp", step))
    ids = lax.dynamic_slice_in_dim(route_ids, place * height, height, 0)
    route = lax.dynamic_slice_in_dim(route_weights, place * height, height, 0)
    table = route_table(ids, route, local * wide_size)
    table = jnp.pad(table, ((0, 0), (0, LANES // 2 - table.shape[1])))
    high = table.astype(jnp.bfloat16)
    low = (table - high.astype(jnp.float32)).astype(jnp.bfloat16)
    block = jnp.concatenate(pieces + [high, low], axis=1)
    weights = load_weights(gate_proj, up_proj, down_proj, block, scalars)
    blocks = gathered(block, "wide")
    half_way = wide_size // 2
    order = [k for k in range(1, wide_size)] + [0]
    chunks = [order[i : i + half_way] for i in range(0, wide_size, half_way)] if half_way else [[0]]
    others = [flip(b, "rep", 1) for b in blocks]
    summed = jnp.zeros((height, cols * groups), jnp.float32)
    for chunk in chunks:
        mine, other = chunk_gradient(
            scalars, [blocks[k] for k in chunk], [others[k] for k in chunk], weights, groups
        )
        kinds = [jnp.bfloat16 if k else jnp.float32 for k in chunk]
        for k, part in zip(chunk, join(mine, flip(other, "rep", 1), kinds)):
            if k:
                part = flip(part, "wide", k)
                part = part.astype(jnp.float32)
            summed = summed + part
    summed = summed.astype(jnp.bfloat16)
    pieces = []
    for step in range(groups):
        piece = summed[:, step * cols : (step + 1) * cols]
        pieces.append(piece if step == 0 else flip(piece, "grp", step))
    bit = 1
    while bit < groups:
        swap = (place & bit) != 0
        pieces = [jnp.where(swap, pieces[k ^ bit], pieces[k]) for k in range(groups)]
        bit *= 2
    return jnp.concatenate(pieces, axis=0)


def shards(hidden_in, grad_out, route_ids, route_weights, gate_proj, up_proj, down_proj):
    wide_size, groups = lax.axis_size("wide"), lax.axis_size("grp")
    experts = gate_proj.shape[0] * wide_size
    fanout = route_ids.shape[1]
    powers = all(n & (n - 1) == 0 for n in (wide_size, groups))
    dense = powers and experts <= 2 * fanout and 2 * experts <= LANES and lax.axis_size("rep") == 2
    path = dense_shards if dense else routed_shards
    return path(
        hidden_in, grad_out, route_ids, route_weights, gate_proj, up_proj, down_proj
    )


def solution(mesh):
    in_specs = (
        P(("wide", "rep"), "grp"),
        P(("wide", "rep"), "grp"),
        P(("wide", "rep"), None),
        P(("wide", "rep"), None),
        P("wide", None, "rep"),
        P("wide", None, "rep"),
        P("wide", "rep", None),
    )
    out_specs = P(("wide", "rep"), "grp")
    return jax.shard_map(
        shards, mesh=mesh, in_specs=in_specs, out_specs=out_specs, check_vma=False
    )
```

```python
import jax
import jax.numpy as jnp
from jax import lax
from jax.experimental import pallas as pl
from jax.experimental.pallas import tpu as pltpu
from jax.sharding import PartitionSpec as P


def expert_back(stacked, gate_mat, up_mat, down_mat):
    inputs = stacked[0]
    scaled = stacked[1]
    pre_gate = jnp.einsum("wecd,edf->wecf", inputs, gate_mat, preferred_element_type=jnp.float32)
    pre_up = jnp.einsum("wecd,edf->wecf", inputs, up_mat, preferred_element_type=jnp.float32)
    back_hidden = jnp.einsum("wecd,efd->wecf", scaled, down_mat, preferred_element_type=jnp.float32)
    gate_sig = jax.nn.sigmoid(pre_gate)
    d_gate = (back_hidden * pre_up * gate_sig * (1.0 + pre_gate * (1.0 - gate_sig))).astype(
        jnp.bfloat16
    )
    d_up = (back_hidden * pre_gate * gate_sig).astype(jnp.bfloat16)
    first_term = jnp.einsum("wecf,edf->wecd", d_gate, gate_mat, preferred_element_type=jnp.float32)
    return first_term + jnp.einsum(
        "wecf,edf->wecd", d_up, up_mat, preferred_element_type=jnp.float32
    )


def slot_ranks(pair_ids, experts):
    pairs = pair_ids.shape[0]
    block = 128
    nblocks = pairs // block
    onehot = (pair_ids[:, None] == jnp.arange(experts, dtype=jnp.int32)[None, :]).astype(
        jnp.bfloat16
    )
    onehot = onehot.reshape(nblocks, block, experts)
    lower = (
        lax.broadcasted_iota(jnp.int32, (block, block), 0)
        > lax.broadcasted_iota(jnp.int32, (block, block), 1)
    ).astype(jnp.bfloat16)
    within = jnp.einsum("ij,bje->bie", lower, onehot, preferred_element_type=jnp.float32)
    totals = jnp.sum(onehot.astype(jnp.float32), axis=1)
    before = jnp.cumsum(totals, axis=0) - totals
    counted = jnp.sum((within + before[:, None, :]) * onehot.astype(jnp.float32), axis=2)
    return counted.reshape(pairs).astype(jnp.int32)


def routed_shards(hidden_in, grad_out, route_ids, route_weights, gate_proj, up_proj, down_proj):
    tok_rows, local_cols = hidden_in.shape
    fanout = route_ids.shape[1]
    wide_size = lax.axis_size("wide")
    groups = lax.axis_size("grp")
    local_experts = gate_proj.shape[0]
    experts = local_experts * wide_size
    capacity = groups * max(1, 3 * tok_rows * fanout // (2 * experts * groups))
    pair_ids = route_ids.reshape(-1)
    slot_rank = slot_ranks(pair_ids, experts)
    position = pair_ids * capacity + slot_rank
    token_ids = jnp.arange(tok_rows * fanout, dtype=jnp.int32) // fanout
    pair_inputs = hidden_in[token_ids]
    pair_scaled = (
        route_weights.reshape(-1)[:, None] * grad_out[token_ids].astype(jnp.float32)
    ).astype(jnp.bfloat16)
    blank_rows = jnp.zeros((experts * capacity, local_cols), jnp.bfloat16)
    outgoing = jnp.stack(
        [blank_rows.at[position].set(pair_inputs), blank_rows.at[position].set(pair_scaled)]
    )
    outgoing = outgoing.reshape(2, wide_size, local_experts, capacity, local_cols)
    received = lax.all_to_all(
        lax.all_to_all(outgoing, "wide", split_axis=1, concat_axis=1, tiled=True),
        "grp",
        split_axis=3,
        concat_axis=4,
        tiled=True,
    )
    full_gate, full_up, full_down = (
        lax.all_gather(gate_proj, "rep", axis=2, tiled=True),
        lax.all_gather(up_proj, "rep", axis=2, tiled=True),
        lax.all_gather(down_proj, "rep", axis=1, tiled=True),
    )
    summed = expert_back(received, full_gate, full_up, full_down)
    returned = lax.all_to_all(
        lax.all_to_all(
            summed.astype(jnp.bfloat16), "wide", split_axis=0, concat_axis=0, tiled=True
        ),
        "grp",
        split_axis=3,
        concat_axis=2,
        tiled=True,
    )
    flat_rows = returned.reshape(experts * capacity, local_cols)
    picked = flat_rows[position].astype(jnp.float32).reshape(tok_rows, fanout, local_cols)
    return jnp.sum(picked, axis=1).astype(jnp.bfloat16)


LANES = 128
VMEM = pl.BlockSpec(memory_space=pltpu.VMEM)
SMEM = pl.BlockSpec(memory_space=pltpu.SMEM)
HBM = pl.BlockSpec(memory_space=pltpu.HBM)


def load_kernel(gate_hbm, up_hbm, down_hbm, after, scalars, both, both_t, down_t, down, sems):
    local, _, half = gate_hbm.shape
    copies = []
    for e in range(local):
        copies.append(
            (
                pltpu.make_async_copy(gate_hbm.at[e], both.at[e, :, :half], sems.at[e, 0]),
                pltpu.make_async_copy(up_hbm.at[e], both.at[e, :, half:], sems.at[e, 1]),
                pltpu.make_async_copy(down_hbm.at[e], down.at[e], sems.at[e, 2]),
            )
        )
        for copy in copies[e]:
            copy.start()
    for e in range(local):
        for copy in copies[e]:
            copy.wait()
        both_t[e] = both[e].T
        down_t[:, e * half : (e + 1) * half] = down[e].T


def load_weights(gate_proj, up_proj, down_proj, after, scalars):
    local, width, half = gate_proj.shape
    size = 6 * local * width * half
    weights = [pltpu.with_memory_space_constraint(w, pltpu.HBM) for w in (gate_proj, up_proj, down_proj)]
    return pl.pallas_call(
        load_kernel,
        in_specs=[HBM] * 3 + [VMEM, SMEM],
        out_specs=[VMEM] * 3,
        out_shape=[
            jax.ShapeDtypeStruct((local, width, 2 * half), jnp.bfloat16),
            jax.ShapeDtypeStruct((local, 2 * half, width), jnp.bfloat16),
            jax.ShapeDtypeStruct((width, local * half), jnp.bfloat16),
        ],
        scratch_shapes=[
            pltpu.VMEM(down_proj.shape, jnp.bfloat16),
            pltpu.SemaphoreType.DMA((local, 3)),
        ],
        compiler_params=pltpu.CompilerParams(vmem_limit_bytes=8 << 20),
        cost_estimate=pl.CostEstimate(flops=0, bytes_accessed=size, transcendentals=0),
        name="load",
    )(*weights, after, scalars)


def chunk_kernel(groups, count, scalars, *refs):
    place, wide = scalars[0], scalars[1]
    blocks = refs[:count]
    both, both_t, down_t, mine_out, other_out, x_rows, g_rows, total = refs[count:]
    local, width, double = both.shape
    half = double // 2
    height = blocks[0].shape[0]
    cols = width // groups
    for number, block in enumerate(blocks):
        rows = slice(number * height, (number + 1) * height)
        for step in range(groups):
            start = pl.multiple_of((place ^ step) * cols, LANES)
            x_rows[rows, pl.ds(start, cols)] = block[:, 2 * step * cols : (2 * step + 1) * cols]
            g_rows[rows, pl.ds(start, cols)] = block[:, (2 * step + 1) * cols : (2 * step + 2) * cols]
    weights = jnp.concatenate([block[:, 2 * width :] for block in blocks], axis=0)
    weights = weights.astype(jnp.float32)
    lane = lax.broadcasted_iota(jnp.int32, weights.shape, 1)
    experts = weights.shape[1] // 2

    for e in range(local):
        named = (lane == wide * local + e) | (lane == wide * local + e + experts)
        route = jnp.sum(jnp.where(named, weights, 0.0), axis=1, keepdims=True)
        pre = jnp.dot(x_rows[...], both[e], preferred_element_type=jnp.float32)
        if e % 2 == 0:
            paired = min(2, local - e)
            back_pair = jnp.dot(
                g_rows[...],
                down_t[:, e * half : (e + paired) * half],
                preferred_element_type=jnp.float32,
            )
        back = route * back_pair[:, (e % 2) * half : (e % 2 + 1) * half]
        pre_gate, pre_up = pre[:, :half], pre[:, half:]
        sig = 1.0 / (1.0 + jnp.exp(-pre_gate))
        d_gate = back * pre_up * sig * (1.0 + pre_gate * (1.0 - sig))
        d_up = back * pre_gate * sig
        hidden = jnp.concatenate([d_gate, d_up], axis=1).astype(jnp.bfloat16)
        term = jnp.dot(hidden, both_t[e], preferred_element_type=jnp.float32)
        if e == 0:
            total[...] = term
        else:
            total[...] += term
    slots = count // 2
    for out, core in ((mine_out, scalars[2]), (other_out, 1 - scalars[2])):
        for index in range(groups // 2):
            start = pl.multiple_of((place ^ (core * (groups - 1)) ^ index) * cols, LANES)
            for slot in range(slots):
                for rep in range(2):
                    first = ((scalars[2] ^ rep) * slots + slot) * height
                    part = total[pl.ds(pl.multiple_of(first, height), height), pl.ds(start, cols)]
                    out[slot, index, rep * height : (rep + 1) * height, :] = part.astype(out.dtype)


def chunk_gradient(scalars, mine, other, weights, groups):
    local, width, double = weights[0].shape
    slots, height = len(mine), mine[0].shape[0]
    rows = 2 * slots * height
    shape = (slots, groups // 2, 2 * height, width // groups)
    return pl.pallas_call(
        lambda *refs: chunk_kernel(groups, 2 * slots, *refs),
        in_specs=[SMEM] + [VMEM] * (2 * slots + 3),
        out_specs=[VMEM, VMEM],
        out_shape=[
            jax.ShapeDtypeStruct(shape, jnp.float32),
            jax.ShapeDtypeStruct(shape, jnp.bfloat16),
        ],
        scratch_shapes=[
            pltpu.VMEM((rows, width), jnp.bfloat16),
            pltpu.VMEM((rows, width), jnp.bfloat16),
            pltpu.VMEM((rows, width), jnp.float32),
        ],
        compiler_params=pltpu.CompilerParams(vmem_limit_bytes=16 * rows * width),
        cost_estimate=pl.CostEstimate(
            flops=10 * 256 * width * (double // 2) * local // 2,
            bytes_accessed=4 * rows * width,
            transcendentals=rows * (double // 2) * local,
        ),
        name="chunk",
    )(scalars, *mine, *other, *weights)


def join_kernel(kinds, mine, swapped, *outs):
    for slot, (_, cut) in enumerate(kinds):
        part = mine[slot] + swapped[slot].astype(jnp.float32)
        for index in range(part.shape[0] if cut else 1):
            out, outs = outs[0], outs[1:]
            out[...] = (part[index] if cut else part).astype(out.dtype)


def join(mine, swapped, kinds):
    shape = mine.shape[1:]
    shapes = []
    for kind, cut in kinds:
        shapes += [jax.ShapeDtypeStruct(shape[1:], kind)] * shape[0] if cut else [jax.ShapeDtypeStruct(shape, kind)]
    outs = pl.pallas_call(
        lambda *refs: join_kernel(kinds, *refs),
        in_specs=[VMEM] * 2,
        out_specs=[VMEM] * len(shapes),
        out_shape=shapes,
        compiler_params=pltpu.CompilerParams(vmem_limit_bytes=1 << 20),
        name="join",
    )(mine, swapped)
    slots = []
    for _, cut in kinds:
        number = shape[0] if cut else 1
        slots.append(outs[:number])
        outs = outs[number:]
    return slots


def flip(array, axis, step):
    size = lax.axis_size(axis)
    return lax.ppermute(array, axis, [(i, i ^ step) for i in range(size)])


def straight(array, wide_step, index):
    wide_size, groups = lax.axis_size("wide"), lax.axis_size("grp")
    pairs = []
    for w in range(wide_size):
        for g in range(groups):
            for r in range(2):
                target = (w ^ wide_step) * groups + (g ^ (r * (groups - 1)) ^ index)
                pairs.append(((w * groups + g) * 2 + r, target * 2 + r))
    return lax.ppermute(array, ("wide", "grp", "rep"), pairs)


def route_table(route_ids, route_weights, experts):
    chosen = route_ids[:, :, None] == jnp.arange(experts, dtype=jnp.int32)[None, None, :]
    return jnp.sum(jnp.where(chosen, route_weights[:, :, None], 0.0), axis=1)


def gathered(block, axis):
    size = lax.axis_size(axis)
    parts = {0: block}
    step = size // 2
    while step:
        for k in sorted(parts):
            parts[k | step] = flip(parts[k], axis, step)
        step //= 2
    return [parts[k] for k in range(size)]


def dense_shards(hidden_in, grad_out, route_ids, route_weights, gate_proj, up_proj, down_proj):
    tok_rows, _ = hidden_in.shape
    wide_size = lax.axis_size("wide")
    groups = lax.axis_size("grp")
    local = gate_proj.shape[0]
    height = tok_rows // groups
    place = lax.axis_index("grp").astype(jnp.int32)
    wide = lax.axis_index("wide").astype(jnp.int32)
    rep = lax.axis_index("rep").astype(jnp.int32)
    scalars = jnp.stack([place, wide, rep])

    pieces = []
    for step in range(groups):
        first = (place ^ step) * height
        piece = jnp.concatenate(
            [lax.dynamic_slice_in_dim(a, first, height, 0) for a in (hidden_in, grad_out)], axis=1
        )
        pieces.append(piece if step == 0 else flip(piece, "grp", step))
    ids = lax.dynamic_slice_in_dim(route_ids, place * height, height, 0)
    route = lax.dynamic_slice_in_dim(route_weights, place * height, height, 0)
    table = route_table(ids, route, local * wide_size)
    table = jnp.pad(table, ((0, 0), (0, LANES // 2 - table.shape[1])))
    high = table.astype(jnp.bfloat16)
    low = (table - high.astype(jnp.float32)).astype(jnp.bfloat16)
    block = jnp.concatenate(pieces + [high, low], axis=1)
    weights = load_weights(gate_proj, up_proj, down_proj, block, scalars)
    blocks = gathered(block, "wide")
    half_way = wide_size // 2
    last = wide_size - 1
    order = [k for k in range(1, wide_size)] + [0]
    chunks = [order[i : i + half_way] for i in range(0, wide_size, half_way)]
    others = []
    for k in range(wide_size):
        others.append(flip(blocks[k], "rep", 1))
    near = None
    for chunk in chunks:
        mine, other = chunk_gradient(
            scalars, [blocks[k] for k in chunk], [others[k] for k in chunk], weights, groups
        )
        swapped = flip(other, "rep", 1)
        kinds = [(jnp.bfloat16 if k else jnp.float32, k == last) for k in chunk]
        for k, parts in zip(chunk, join(mine, swapped, kinds)):
            if k == last:
                far = []
                for index, part in enumerate(parts):
                    far.append(straight(part, k, index))
                continue
            part = parts[0]
            if k:
                part = flip(part, "wide", k)
            part = part.astype(jnp.float32)
            near = part if near is None else part + near
    first_core = rep == 0
    keep, give = [], []
    for index in range(groups // 2):
        piece = straight(near[index].astype(jnp.bfloat16), 0, index)
        piece = piece.astype(jnp.float32) + far[index].astype(jnp.float32)
        piece = piece.astype(jnp.bfloat16)
        keep.append(jnp.where(first_core, piece[:height], piece[height:]))
        give.append(jnp.where(first_core, piece[height:], piece[:height]))
    taken = flip(jnp.concatenate(give[::-1], axis=0), "rep", 1)
    pieces = keep + [taken[i * height : (i + 1) * height] for i in range(groups // 2)]
    place = place ^ (rep * (groups - 1))
    bit = 1
    while bit < groups:
        swap = (place & bit) != 0
        pieces = [jnp.where(swap, pieces[k ^ bit], pieces[k]) for k in range(groups)]
        bit *= 2
    return jnp.concatenate(pieces, axis=0)


def shards(hidden_in, grad_out, route_ids, route_weights, gate_proj, up_proj, down_proj):
    wide_size, groups = lax.axis_size("wide"), lax.axis_size("grp")
    experts = gate_proj.shape[0] * wide_size
    fanout = route_ids.shape[1]
    powers = all(n > 1 and n & (n - 1) == 0 for n in (wide_size, groups))
    dense = powers and experts <= 2 * fanout and 2 * experts <= LANES and lax.axis_size("rep") == 2
    path = dense_shards if dense else routed_shards
    return path(
        hidden_in, grad_out, route_ids, route_weights, gate_proj, up_proj, down_proj
    )


def solution(mesh):
    in_specs = (
        P(("wide", "rep"), "grp"),
        P(("wide", "rep"), "grp"),
        P(("wide", "rep"), None),
        P(("wide", "rep"), None),
        P("wide", None, "rep"),
        P("wide", None, "rep"),
        P("wide", "rep", None),
    )
    out_specs = P(("wide", "rep"), "grp")
    return jax.shard_map(
        shards, mesh=mesh, in_specs=in_specs, out_specs=out_specs, check_vma=False
    )
```

```python
import jax
import jax.numpy as jnp
from jax import lax
from jax.experimental import pallas as pl
from jax.experimental.pallas import tpu as pltpu
from jax.sharding import PartitionSpec as P


def expert_back(stacked, gate_mat, up_mat, down_mat):
    inputs = stacked[0]
    scaled = stacked[1]
    pre_gate = jnp.einsum("wecd,edf->wecf", inputs, gate_mat, preferred_element_type=jnp.float32)
    pre_up = jnp.einsum("wecd,edf->wecf", inputs, up_mat, preferred_element_type=jnp.float32)
    back_hidden = jnp.einsum("wecd,efd->wecf", scaled, down_mat, preferred_element_type=jnp.float32)
    gate_sig = jax.nn.sigmoid(pre_gate)
    d_gate = (back_hidden * pre_up * gate_sig * (1.0 + pre_gate * (1.0 - gate_sig))).astype(
        jnp.bfloat16
    )
    d_up = (back_hidden * pre_gate * gate_sig).astype(jnp.bfloat16)
    first_term = jnp.einsum("wecf,edf->wecd", d_gate, gate_mat, preferred_element_type=jnp.float32)
    return first_term + jnp.einsum(
        "wecf,edf->wecd", d_up, up_mat, preferred_element_type=jnp.float32
    )


def slot_ranks(pair_ids, experts):
    pairs = pair_ids.shape[0]
    block = 128
    nblocks = pairs // block
    onehot = (pair_ids[:, None] == jnp.arange(experts, dtype=jnp.int32)[None, :]).astype(
        jnp.bfloat16
    )
    onehot = onehot.reshape(nblocks, block, experts)
    lower = (
        lax.broadcasted_iota(jnp.int32, (block, block), 0)
        > lax.broadcasted_iota(jnp.int32, (block, block), 1)
    ).astype(jnp.bfloat16)
    within = jnp.einsum("ij,bje->bie", lower, onehot, preferred_element_type=jnp.float32)
    totals = jnp.sum(onehot.astype(jnp.float32), axis=1)
    before = jnp.cumsum(totals, axis=0) - totals
    counted = jnp.sum((within + before[:, None, :]) * onehot.astype(jnp.float32), axis=2)
    return counted.reshape(pairs).astype(jnp.int32)


def routed_shards(hidden_in, grad_out, route_ids, route_weights, gate_proj, up_proj, down_proj):
    tok_rows, local_cols = hidden_in.shape
    fanout = route_ids.shape[1]
    wide_size = lax.axis_size("wide")
    groups = lax.axis_size("grp")
    local_experts = gate_proj.shape[0]
    experts = local_experts * wide_size
    capacity = groups * max(1, 3 * tok_rows * fanout // (2 * experts * groups))
    pair_ids = route_ids.reshape(-1)
    slot_rank = slot_ranks(pair_ids, experts)
    position = pair_ids * capacity + slot_rank
    token_ids = jnp.arange(tok_rows * fanout, dtype=jnp.int32) // fanout
    pair_inputs = hidden_in[token_ids]
    pair_scaled = (
        route_weights.reshape(-1)[:, None] * grad_out[token_ids].astype(jnp.float32)
    ).astype(jnp.bfloat16)
    blank_rows = jnp.zeros((experts * capacity, local_cols), jnp.bfloat16)
    outgoing = jnp.stack(
        [blank_rows.at[position].set(pair_inputs), blank_rows.at[position].set(pair_scaled)]
    )
    outgoing = outgoing.reshape(2, wide_size, local_experts, capacity, local_cols)
    received = lax.all_to_all(
        lax.all_to_all(outgoing, "wide", split_axis=1, concat_axis=1, tiled=True),
        "grp",
        split_axis=3,
        concat_axis=4,
        tiled=True,
    )
    full_gate, full_up, full_down = (
        lax.all_gather(gate_proj, "rep", axis=2, tiled=True),
        lax.all_gather(up_proj, "rep", axis=2, tiled=True),
        lax.all_gather(down_proj, "rep", axis=1, tiled=True),
    )
    summed = expert_back(received, full_gate, full_up, full_down)
    returned = lax.all_to_all(
        lax.all_to_all(
            summed.astype(jnp.bfloat16), "wide", split_axis=0, concat_axis=0, tiled=True
        ),
        "grp",
        split_axis=3,
        concat_axis=2,
        tiled=True,
    )
    flat_rows = returned.reshape(experts * capacity, local_cols)
    picked = flat_rows[position].astype(jnp.float32).reshape(tok_rows, fanout, local_cols)
    return jnp.sum(picked, axis=1).astype(jnp.bfloat16)


LANES = 128
VMEM = pl.BlockSpec(memory_space=pltpu.VMEM)
SMEM = pl.BlockSpec(memory_space=pltpu.SMEM)
HBM = pl.BlockSpec(memory_space=pltpu.HBM)


def load_kernel(gate_hbm, up_hbm, down_hbm, after, scalars, both, both_t, down, sems):
    local, _, half = gate_hbm.shape
    halves = (pl.ds(0, half), pl.ds(half, half))
    copies, down_copies = [], []
    for e in range(local):
        for number, source in enumerate((gate_hbm, up_hbm)):
            place = both.at[e, :, halves[number]]
            copies.append(pltpu.make_async_copy(source.at[e], place, sems.at[e, number]))
        place = down.at[pl.ds(e * half, half), :]
        down_copies.append(pltpu.make_async_copy(down_hbm.at[e], place, sems.at[e, 2]))
    for copy in copies + down_copies:
        copy.start()
    for number, copy in enumerate(copies):
        copy.wait()
        e, side = divmod(number, 2)
        both_t[e, side * half : (side + 1) * half] = both[e, :, side * half : (side + 1) * half].T
    for copy in down_copies:
        copy.wait()


def load_weights(gate_proj, up_proj, down_proj, after, scalars):
    local, width, half = gate_proj.shape
    size = 6 * local * width * half
    weights = [pltpu.with_memory_space_constraint(w, pltpu.HBM) for w in (gate_proj, up_proj, down_proj)]
    return pl.pallas_call(
        load_kernel,
        in_specs=[HBM] * 3 + [VMEM, SMEM],
        out_specs=[VMEM] * 3,
        out_shape=[
            jax.ShapeDtypeStruct((local, width, 2 * half), jnp.bfloat16),
            jax.ShapeDtypeStruct((local, 2 * half, width), jnp.bfloat16),
            jax.ShapeDtypeStruct((local * half, width), jnp.bfloat16),
        ],
        scratch_shapes=[pltpu.SemaphoreType.DMA((local, 3))],
        compiler_params=pltpu.CompilerParams(vmem_limit_bytes=8 << 20),
        cost_estimate=pl.CostEstimate(flops=0, bytes_accessed=size, transcendentals=0),
        name="load",
    )(*weights, after, scalars)


def chunk_kernel(groups, count, turn, scalars, *refs):
    place, wide = scalars[0], scalars[1]
    blocks = refs[:count]
    if turn:
        both, both_t, down, mine_out, other_out, down_t, x_rows, g_rows, total = refs[count:]
    else:
        both, both_t, down_t, mine_out, other_out, x_rows, g_rows, total = refs[count:]
    local, width, double = both.shape
    half = double // 2
    height = blocks[0].shape[0]
    cols = width // groups
    for number, block in enumerate(blocks):
        rows = slice(number * height, (number + 1) * height)
        for step in range(groups):
            start = pl.multiple_of((place ^ step) * cols, LANES)
            x_rows[rows, pl.ds(start, cols)] = block[:, 2 * step * cols : (2 * step + 1) * cols]
            g_rows[rows, pl.ds(start, cols)] = block[:, (2 * step + 1) * cols : (2 * step + 2) * cols]
    weights = jnp.concatenate([block[:, 2 * width :] for block in blocks], axis=0)
    weights = weights.astype(jnp.float32)
    lane = lax.broadcasted_iota(jnp.int32, weights.shape, 1)
    experts = weights.shape[1] // 2

    for e in range(local):
        named = (lane == wide * local + e) | (lane == wide * local + e + experts)
        route = jnp.sum(jnp.where(named, weights, 0.0), axis=1, keepdims=True)
        if e % 2 == 0:
            pair = slice(e * half, (e + min(2, local - e)) * half)
            if turn:
                down_t[:, pair] = down[pair].T
            back_pair = jnp.dot(
                g_rows[...],
                down_t[:, pair],
                preferred_element_type=jnp.float32,
            )
        pre = jnp.dot(x_rows[...], both[e], preferred_element_type=jnp.float32)
        back = route * back_pair[:, (e % 2) * half : (e % 2 + 1) * half]
        pre_gate, pre_up = pre[:, :half], pre[:, half:]
        sig = 1.0 / (1.0 + jnp.exp(-pre_gate))
        d_gate = back * pre_up * sig * (1.0 + pre_gate * (1.0 - sig))
        d_up = back * pre_gate * sig
        hidden = jnp.concatenate([d_gate, d_up], axis=1).astype(jnp.bfloat16)
        term = jnp.dot(hidden, both_t[e], preferred_element_type=jnp.float32)
        if e == 0:
            total[...] = term
        else:
            total[...] += term
    slots = count // 2
    for out, core in ((mine_out, scalars[2]), (other_out, 1 - scalars[2])):
        for index in range(groups // 2):
            start = pl.multiple_of((place ^ (core * (groups - 1)) ^ index) * cols, LANES)
            for slot in range(slots):
                for rep in range(2):
                    first = ((scalars[2] ^ rep) * slots + slot) * height
                    part = total[pl.ds(pl.multiple_of(first, height), height), pl.ds(start, cols)]
                    out[slot, index, rep * height : (rep + 1) * height, :] = part.astype(out.dtype)


def chunk_gradient(scalars, mine, other, weights, groups, turn):
    local, width, double = weights[0].shape
    slots, height = len(mine), mine[0].shape[0]
    rows = 2 * slots * height
    shape = (slots, groups // 2, 2 * height, width // groups)
    return pl.pallas_call(
        lambda *refs: chunk_kernel(groups, 2 * slots, turn, *refs),
        in_specs=[SMEM] + [VMEM] * (2 * slots + 3),
        out_specs=[VMEM] * (3 if turn else 2),
        out_shape=[
            jax.ShapeDtypeStruct(shape, jnp.float32),
            jax.ShapeDtypeStruct(shape, jnp.bfloat16),
        ]
        + [jax.ShapeDtypeStruct(weights[2].shape[::-1], jnp.bfloat16)] * turn,
        scratch_shapes=[
            pltpu.VMEM((rows, width), jnp.bfloat16),
            pltpu.VMEM((rows, width), jnp.bfloat16),
            pltpu.VMEM((rows, width), jnp.float32),
        ],
        compiler_params=pltpu.CompilerParams(vmem_limit_bytes=16 * rows * width),
        cost_estimate=pl.CostEstimate(
            flops=10 * 256 * width * (double // 2) * local // 2,
            bytes_accessed=4 * rows * width,
            transcendentals=rows * (double // 2) * local,
        ),
        name="chunk",
    )(scalars, *mine, *other, *weights)


def join_kernel(kinds, mine, swapped, *outs):
    for slot, (_, cut) in enumerate(kinds):
        part = mine[slot] + swapped[slot].astype(jnp.float32)
        for index in range(part.shape[0] if cut else 1):
            out, outs = outs[0], outs[1:]
            out[...] = (part[index] if cut else part).astype(out.dtype)


def join(mine, swapped, kinds):
    shape = mine.shape[1:]
    shapes = []
    for kind, cut in kinds:
        shapes += [jax.ShapeDtypeStruct(shape[1:], kind)] * shape[0] if cut else [jax.ShapeDtypeStruct(shape, kind)]
    outs = pl.pallas_call(
        lambda *refs: join_kernel(kinds, *refs),
        in_specs=[VMEM] * 2,
        out_specs=[VMEM] * len(shapes),
        out_shape=shapes,
        compiler_params=pltpu.CompilerParams(vmem_limit_bytes=1 << 20),
        name="join",
    )(mine, swapped)
    slots = []
    for _, cut in kinds:
        number = shape[0] if cut else 1
        slots.append(outs[:number])
        outs = outs[number:]
    return slots


def flip(array, axis, step):
    size = lax.axis_size(axis)
    return lax.ppermute(array, axis, [(i, i ^ step) for i in range(size)])


def straight(array, wide_step, index):
    wide_size, groups = lax.axis_size("wide"), lax.axis_size("grp")
    pairs = []
    for w in range(wide_size):
        for g in range(groups):
            for r in range(2):
                target = (w ^ wide_step) * groups + (g ^ (r * (groups - 1)) ^ index)
                pairs.append(((w * groups + g) * 2 + r, target * 2 + r))
    return lax.ppermute(array, ("wide", "grp", "rep"), pairs)


def route_table(route_ids, route_weights, experts):
    chosen = route_ids[:, :, None] == jnp.arange(experts, dtype=jnp.int32)[None, None, :]
    return jnp.sum(jnp.where(chosen, route_weights[:, :, None], 0.0), axis=1)


def gathered(block, far_block, axis):
    size = lax.axis_size(axis)
    parts = {0: block, size // 2: far_block}
    step = size // 4
    while step:
        for k in sorted(parts):
            parts[k | step] = flip(parts[k], axis, step)
        step //= 2
    return [parts[k] for k in range(size)]


def dense_shards(hidden_in, grad_out, route_ids, route_weights, gate_proj, up_proj, down_proj):
    tok_rows, _ = hidden_in.shape
    wide_size = lax.axis_size("wide")
    groups = lax.axis_size("grp")
    local = gate_proj.shape[0]
    height = tok_rows // groups
    place = lax.axis_index("grp").astype(jnp.int32)
    wide = lax.axis_index("wide").astype(jnp.int32)
    rep = lax.axis_index("rep").astype(jnp.int32)
    scalars = jnp.stack([place, wide, rep])

    pieces = []
    for step in range(groups):
        first = (place ^ step) * height
        piece = jnp.concatenate(
            [lax.dynamic_slice_in_dim(a, first, height, 0) for a in (hidden_in, grad_out)], axis=1
        )
        pieces.append(piece if step == 0 else flip(piece, "grp", step))
    half_way = wide_size // 2
    early = flip(pieces[0], "wide", half_way)
    ids = lax.dynamic_slice_in_dim(route_ids, place * height, height, 0)
    route = lax.dynamic_slice_in_dim(route_weights, place * height, height, 0)
    table = route_table(ids, route, local * wide_size)
    table = jnp.pad(table, ((0, 0), (0, LANES // 2 - table.shape[1])))
    high = table.astype(jnp.bfloat16)
    low = (table - high.astype(jnp.float32)).astype(jnp.bfloat16)
    rest = jnp.concatenate(pieces[1:] + [high, low], axis=1)
    far_block = jnp.concatenate([early, flip(rest, "wide", half_way)], axis=1)
    block = jnp.concatenate([pieces[0], rest], axis=1)
    weights = load_weights(gate_proj, up_proj, down_proj, block, scalars)
    blocks = gathered(block, far_block, "wide")
    chunks = [list(range(first, wide_size, 2))[::-1] for first in (0, 1)]
    others = []
    for k in range(wide_size):
        others.append(flip(blocks[k], "rep", 1))
    near, far = None, [[] for _ in range(groups // 2)]
    for number, chunk in enumerate(chunks):
        mine, other, *turned = chunk_gradient(
            scalars,
            [blocks[k] for k in chunk],
            [others[k] for k in chunk],
            weights,
            groups,
            turn=number == 0,
        )
        weights = list(weights[:2]) + (turned or [weights[2]])
        swapped = flip(other, "rep", 1)
        kinds = [(jnp.bfloat16 if k else jnp.float32, k == wide_size - 1) for k in chunk]
        for k, parts in zip(chunk, join(mine, swapped, kinds)):
            if k == wide_size - 1:
                for index, part in enumerate(parts):
                    far[index].append(straight(part, k, index))
                continue
            part = parts[0]
            if k:
                part = flip(part, "wide", k)
            part = part.astype(jnp.float32)
            near = part if near is None else part + near
    first_core = rep == 0
    keep, give = [], []
    for index in range(groups // 2):
        piece = straight(near[index].astype(jnp.bfloat16), 0, index)
        piece = piece.astype(jnp.float32)
        for part in far[index]:
            piece = piece + part.astype(jnp.float32)
        piece = piece.astype(jnp.bfloat16)
        keep.append(jnp.where(first_core, piece[:height], piece[height:]))
        give.append(jnp.where(first_core, piece[height:], piece[:height]))
    taken = flip(jnp.concatenate(give[::-1], axis=0), "rep", 1)
    pieces = keep + [taken[i * height : (i + 1) * height] for i in range(groups // 2)]
    place = place ^ (rep * (groups - 1))
    bit = 1
    while bit < groups:
        swap = (place & bit) != 0
        pieces = [jnp.where(swap, pieces[k ^ bit], pieces[k]) for k in range(groups)]
        bit *= 2
    return jnp.concatenate(pieces, axis=0)


def shards(hidden_in, grad_out, route_ids, route_weights, gate_proj, up_proj, down_proj):
    wide_size, groups = lax.axis_size("wide"), lax.axis_size("grp")
    experts = gate_proj.shape[0] * wide_size
    fanout = route_ids.shape[1]
    powers = all(n > 1 and n & (n - 1) == 0 for n in (wide_size, groups))
    dense = powers and experts <= 2 * fanout and 2 * experts <= LANES and lax.axis_size("rep") == 2
    path = dense_shards if dense else routed_shards
    return path(
        hidden_in, grad_out, route_ids, route_weights, gate_proj, up_proj, down_proj
    )


def solution(mesh):
    in_specs = (
        P(("wide", "rep"), "grp"),
        P(("wide", "rep"), "grp"),
        P(("wide", "rep"), None),
        P(("wide", "rep"), None),
        P("wide", None, "rep"),
        P("wide", None, "rep"),
        P("wide", "rep", None),
    )
    out_specs = P(("wide", "rep"), "grp")
    return jax.shard_map(
        shards, mesh=mesh, in_specs=in_specs, out_specs=out_specs, check_vma=False
    )
```

```python
import jax
import jax.numpy as jnp
from jax import lax
from jax.experimental import pallas as pl
from jax.experimental.pallas import tpu as pltpu
from jax.sharding import PartitionSpec as P


def expert_back(stacked, gate_mat, up_mat, down_mat):
    inputs = stacked[0]
    scaled = stacked[1]
    pre_gate = jnp.einsum("wecd,edf->wecf", inputs, gate_mat, preferred_element_type=jnp.float32)
    pre_up = jnp.einsum("wecd,edf->wecf", inputs, up_mat, preferred_element_type=jnp.float32)
    back_hidden = jnp.einsum("wecd,efd->wecf", scaled, down_mat, preferred_element_type=jnp.float32)
    gate_sig = jax.nn.sigmoid(pre_gate)
    d_gate = (back_hidden * pre_up * gate_sig * (1.0 + pre_gate * (1.0 - gate_sig))).astype(
        jnp.bfloat16
    )
    d_up = (back_hidden * pre_gate * gate_sig).astype(jnp.bfloat16)
    first_term = jnp.einsum("wecf,edf->wecd", d_gate, gate_mat, preferred_element_type=jnp.float32)
    return first_term + jnp.einsum(
        "wecf,edf->wecd", d_up, up_mat, preferred_element_type=jnp.float32
    )


def slot_ranks(pair_ids, experts):
    pairs = pair_ids.shape[0]
    block = 128
    nblocks = pairs // block
    onehot = (pair_ids[:, None] == jnp.arange(experts, dtype=jnp.int32)[None, :]).astype(
        jnp.bfloat16
    )
    onehot = onehot.reshape(nblocks, block, experts)
    lower = (
        lax.broadcasted_iota(jnp.int32, (block, block), 0)
        > lax.broadcasted_iota(jnp.int32, (block, block), 1)
    ).astype(jnp.bfloat16)
    within = jnp.einsum("ij,bje->bie", lower, onehot, preferred_element_type=jnp.float32)
    totals = jnp.sum(onehot.astype(jnp.float32), axis=1)
    before = jnp.cumsum(totals, axis=0) - totals
    counted = jnp.sum((within + before[:, None, :]) * onehot.astype(jnp.float32), axis=2)
    return counted.reshape(pairs).astype(jnp.int32)


def routed_shards(hidden_in, grad_out, route_ids, route_weights, gate_proj, up_proj, down_proj):
    tok_rows, local_cols = hidden_in.shape
    fanout = route_ids.shape[1]
    wide_size = lax.axis_size("wide")
    groups = lax.axis_size("grp")
    local_experts = gate_proj.shape[0]
    experts = local_experts * wide_size
    capacity = groups * max(1, 3 * tok_rows * fanout // (2 * experts * groups))
    pair_ids = route_ids.reshape(-1)
    slot_rank = slot_ranks(pair_ids, experts)
    position = pair_ids * capacity + slot_rank
    token_ids = jnp.arange(tok_rows * fanout, dtype=jnp.int32) // fanout
    pair_inputs = hidden_in[token_ids]
    pair_scaled = (
        route_weights.reshape(-1)[:, None] * grad_out[token_ids].astype(jnp.float32)
    ).astype(jnp.bfloat16)
    blank_rows = jnp.zeros((experts * capacity, local_cols), jnp.bfloat16)
    outgoing = jnp.stack(
        [blank_rows.at[position].set(pair_inputs), blank_rows.at[position].set(pair_scaled)]
    )
    outgoing = outgoing.reshape(2, wide_size, local_experts, capacity, local_cols)
    received = lax.all_to_all(
        lax.all_to_all(outgoing, "wide", split_axis=1, concat_axis=1, tiled=True),
        "grp",
        split_axis=3,
        concat_axis=4,
        tiled=True,
    )
    full_gate, full_up, full_down = (
        lax.all_gather(gate_proj, "rep", axis=2, tiled=True),
        lax.all_gather(up_proj, "rep", axis=2, tiled=True),
        lax.all_gather(down_proj, "rep", axis=1, tiled=True),
    )
    summed = expert_back(received, full_gate, full_up, full_down)
    returned = lax.all_to_all(
        lax.all_to_all(
            summed.astype(jnp.bfloat16), "wide", split_axis=0, concat_axis=0, tiled=True
        ),
        "grp",
        split_axis=3,
        concat_axis=2,
        tiled=True,
    )
    flat_rows = returned.reshape(experts * capacity, local_cols)
    picked = flat_rows[position].astype(jnp.float32).reshape(tok_rows, fanout, local_cols)
    return jnp.sum(picked, axis=1).astype(jnp.bfloat16)


LANES = 128
VMEM = pl.BlockSpec(memory_space=pltpu.VMEM)
SMEM = pl.BlockSpec(memory_space=pltpu.SMEM)
HBM = pl.BlockSpec(memory_space=pltpu.HBM)


def load_kernel(gate_hbm, up_hbm, down_hbm, after, scalars, both, both_t, down, sems):
    local, _, half = gate_hbm.shape
    halves = (pl.ds(0, half), pl.ds(half, half))
    copies, down_copies = [], []
    for e in range(local):
        for number, source in enumerate((gate_hbm, up_hbm)):
            place = both.at[e, :, halves[number]]
            copies.append(pltpu.make_async_copy(source.at[e], place, sems.at[e, number]))
        place = down.at[pl.ds(e * half, half), :]
        down_copies.append(pltpu.make_async_copy(down_hbm.at[e], place, sems.at[e, 2]))
    for copy in copies + down_copies:
        copy.start()
    for number, copy in enumerate(copies):
        copy.wait()
        e, side = divmod(number, 2)
        both_t[e, side * half : (side + 1) * half] = both[e, :, side * half : (side + 1) * half].T
    for copy in down_copies:
        copy.wait()


def load_weights(gate_proj, up_proj, down_proj, after, scalars):
    local, width, half = gate_proj.shape
    size = 6 * local * width * half
    weights = [pltpu.with_memory_space_constraint(w, pltpu.HBM) for w in (gate_proj, up_proj, down_proj)]
    return pl.pallas_call(
        load_kernel,
        in_specs=[HBM] * 3 + [VMEM, SMEM],
        out_specs=[VMEM] * 3,
        out_shape=[
            jax.ShapeDtypeStruct((local, width, 2 * half), jnp.bfloat16),
            jax.ShapeDtypeStruct((local, 2 * half, width), jnp.bfloat16),
            jax.ShapeDtypeStruct((local * half, width), jnp.bfloat16),
        ],
        scratch_shapes=[pltpu.SemaphoreType.DMA((local, 3))],
        compiler_params=pltpu.CompilerParams(vmem_limit_bytes=8 << 20),
        cost_estimate=pl.CostEstimate(flops=0, bytes_accessed=size, transcendentals=0),
        name="load",
    )(*weights, after, scalars)


def chunk_kernel(groups, count, turn, scalars, *refs):
    place, wide = scalars[0], scalars[1]
    blocks = refs[:count]
    if turn:
        both, both_t, down, hidden_out, give_out, down_t, x_rows, g_rows, total = refs[count:]
    else:
        both, both_t, down_t, hidden_out, give_out, x_rows, g_rows, total = refs[count:]
    local, width, double = both.shape
    half = double // 2
    height = blocks[0].shape[0]
    cols = width // groups
    for number, block in enumerate(blocks):
        rows = slice(number * height, (number + 1) * height)
        for step in range(groups):
            start = pl.multiple_of((place ^ step) * cols, LANES)
            x_rows[rows, pl.ds(start, cols)] = block[:, 2 * step * cols : (2 * step + 1) * cols]
            g_rows[rows, pl.ds(start, cols)] = block[:, (2 * step + 1) * cols : (2 * step + 2) * cols]
    weights = jnp.concatenate([block[:, 2 * width :] for block in blocks], axis=0)
    weights = weights.astype(jnp.float32)
    lane = lax.broadcasted_iota(jnp.int32, weights.shape, 1)
    experts = weights.shape[1] // 2

    for e in range(local):
        named = (lane == wide * local + e) | (lane == wide * local + e + experts)
        route = jnp.sum(jnp.where(named, weights, 0.0), axis=1, keepdims=True)
        if e % 2 == 0:
            pair = slice(e * half, (e + min(2, local - e)) * half)
            if turn:
                down_t[:, pair] = down[pair].T
            back_pair = jnp.dot(
                g_rows[...],
                down_t[:, pair],
                preferred_element_type=jnp.float32,
            )
        pre = jnp.dot(x_rows[...], both[e], preferred_element_type=jnp.float32)
        back = route * back_pair[:, (e % 2) * half : (e % 2 + 1) * half]
        pre_gate, pre_up = pre[:, :half], pre[:, half:]
        sig = 1.0 / (1.0 + jnp.exp(-pre_gate))
        d_gate = back * pre_up * sig * (1.0 + pre_gate * (1.0 - sig))
        d_up = back * pre_gate * sig
        hidden = jnp.concatenate([d_gate, d_up], axis=1).astype(jnp.bfloat16)
        hidden_out[e] = hidden
        add_places(scalars, 1 - scalars[2], hidden, both_t, e, total)
    put_places(scalars, total, give_out)


def add_places(scalars, core, hidden, both_t, e, total):
    cols = total.shape[2]
    groups = both_t.shape[2] // cols
    for index in range(total.shape[0]):
        start = (scalars[0] ^ (core * (groups - 1)) ^ index) * cols
        columns = pl.ds(pl.multiple_of(start, LANES), cols)
        term = jnp.dot(hidden, both_t[e, :, columns], preferred_element_type=jnp.float32)
        if e == 0:
            total[index] = term
        else:
            total[index] += term


def put_places(scalars, total, out):
    slots, _, double, _ = out.shape
    height = double // 2
    for index in range(total.shape[0]):
        for slot in range(slots):
            for rep in range(2):
                first = pl.multiple_of(((scalars[2] ^ rep) * slots + slot) * height, height)
                part = total[index, pl.ds(first, height), :]
                out[slot, index, rep * height : (rep + 1) * height, :] = part.astype(out.dtype)


def keep_kernel(scalars, hidden, both_t, keep_out, total):
    for e in range(hidden.shape[0]):
        add_places(scalars, scalars[2], hidden[e], both_t, e, total)
    put_places(scalars, total, keep_out)


def keep_gradient(scalars, hidden, both_t, give):
    local, rows, double = hidden.shape
    _, places, _, cols = give.shape
    return pl.pallas_call(
        keep_kernel,
        in_specs=[SMEM] + [VMEM] * 2,
        out_specs=VMEM,
        out_shape=jax.ShapeDtypeStruct(give.shape, jnp.float32),
        scratch_shapes=[pltpu.VMEM((places, rows, cols), jnp.float32)],
        compiler_params=pltpu.CompilerParams(vmem_limit_bytes=16 * rows * places * cols),
        cost_estimate=pl.CostEstimate(
            flops=2 * rows * double * places * cols * local,
            bytes_accessed=2 * local * rows * double,
            transcendentals=0,
        ),
        name="keep",
    )(scalars, hidden, both_t)


def chunk_gradient(scalars, mine, other, weights, groups, turn):
    local, width, double = weights[0].shape
    slots, height = len(mine), mine[0].shape[0]
    rows = 2 * slots * height
    shape = (slots, groups // 2, 2 * height, width // groups)
    return pl.pallas_call(
        lambda *refs: chunk_kernel(groups, 2 * slots, turn, *refs),
        in_specs=[SMEM] + [VMEM] * (2 * slots + 3),
        out_specs=[VMEM] * (3 if turn else 2),
        out_shape=[
            jax.ShapeDtypeStruct((local, rows, double), jnp.bfloat16),
            jax.ShapeDtypeStruct(shape, jnp.bfloat16),
        ]
        + [jax.ShapeDtypeStruct(weights[2].shape[::-1], jnp.bfloat16)] * turn,
        scratch_shapes=[
            pltpu.VMEM((rows, width), jnp.bfloat16),
            pltpu.VMEM((rows, width), jnp.bfloat16),
            pltpu.VMEM((groups // 2, rows, width // groups), jnp.float32),
        ],
        compiler_params=pltpu.CompilerParams(vmem_limit_bytes=16 * rows * width),
        cost_estimate=pl.CostEstimate(
            flops=10 * 256 * width * (double // 2) * local // 2,
            bytes_accessed=4 * rows * width,
            transcendentals=rows * (double // 2) * local,
        ),
        name="chunk",
    )(scalars, *mine, *other, *weights)


def join_kernel(kinds, mine, swapped, *outs):
    for slot, (_, cut) in enumerate(kinds):
        part = mine[slot] + swapped[slot].astype(jnp.float32)
        for index in range(part.shape[0] if cut else 1):
            out, outs = outs[0], outs[1:]
            out[...] = (part[index] if cut else part).astype(out.dtype)


def join(mine, swapped, kinds):
    shape = mine.shape[1:]
    shapes = []
    for kind, cut in kinds:
        shapes += [jax.ShapeDtypeStruct(shape[1:], kind)] * shape[0] if cut else [jax.ShapeDtypeStruct(shape, kind)]
    outs = pl.pallas_call(
        lambda *refs: join_kernel(kinds, *refs),
        in_specs=[VMEM] * 2,
        out_specs=[VMEM] * len(shapes),
        out_shape=shapes,
        compiler_params=pltpu.CompilerParams(vmem_limit_bytes=1 << 20),
        name="join",
    )(mine, swapped)
    slots = []
    for _, cut in kinds:
        number = shape[0] if cut else 1
        slots.append(outs[:number])
        outs = outs[number:]
    return slots


def flip(array, axis, step):
    size = lax.axis_size(axis)
    return lax.ppermute(array, axis, [(i, i ^ step) for i in range(size)])


def straight(array, wide_step, index):
    wide_size, groups = lax.axis_size("wide"), lax.axis_size("grp")
    pairs = []
    for w in range(wide_size):
        for g in range(groups):
            for r in range(2):
                target = (w ^ wide_step) * groups + (g ^ (r * (groups - 1)) ^ index)
                pairs.append(((w * groups + g) * 2 + r, target * 2 + r))
    return lax.ppermute(array, ("wide", "grp", "rep"), pairs)


def route_table(route_ids, route_weights, experts):
    chosen = route_ids[:, :, None] == jnp.arange(experts, dtype=jnp.int32)[None, None, :]
    return jnp.sum(jnp.where(chosen, route_weights[:, :, None], 0.0), axis=1)


def gathered(block, far_block, axis):
    size = lax.axis_size(axis)
    parts = {0: block, size // 2: far_block}
    step = size // 4
    while step:
        for k in sorted(parts):
            parts[k | step] = flip(parts[k], axis, step)
        step //= 2
    return [parts[k] for k in range(size)]


def dense_shards(hidden_in, grad_out, route_ids, route_weights, gate_proj, up_proj, down_proj):
    tok_rows, _ = hidden_in.shape
    wide_size = lax.axis_size("wide")
    groups = lax.axis_size("grp")
    local = gate_proj.shape[0]
    height = tok_rows // groups
    place = lax.axis_index("grp").astype(jnp.int32)
    wide = lax.axis_index("wide").astype(jnp.int32)
    rep = lax.axis_index("rep").astype(jnp.int32)
    scalars = jnp.stack([place, wide, rep])

    pieces = []
    for step in range(groups):
        first = (place ^ step) * height
        piece = jnp.concatenate(
            [lax.dynamic_slice_in_dim(a, first, height, 0) for a in (hidden_in, grad_out)], axis=1
        )
        pieces.append(piece if step == 0 else flip(piece, "grp", step))
    half_way = wide_size // 2
    early = flip(pieces[0], "wide", half_way)
    ids = lax.dynamic_slice_in_dim(route_ids, place * height, height, 0)
    route = lax.dynamic_slice_in_dim(route_weights, place * height, height, 0)
    table = route_table(ids, route, local * wide_size)
    table = jnp.pad(table, ((0, 0), (0, LANES // 2 - table.shape[1])))
    high = table.astype(jnp.bfloat16)
    low = (table - high.astype(jnp.float32)).astype(jnp.bfloat16)
    rest = jnp.concatenate(pieces[1:] + [high, low], axis=1)
    far_block = jnp.concatenate([early, flip(rest, "wide", half_way)], axis=1)
    block = jnp.concatenate([pieces[0], rest], axis=1)
    weights = load_weights(gate_proj, up_proj, down_proj, block, scalars)
    blocks = gathered(block, far_block, "wide")
    chunks = [list(range(first, wide_size, 2))[::-1] for first in (0, 1)]
    others = []
    for k in range(wide_size):
        others.append(flip(blocks[k], "rep", 1))
    near, far = None, [[] for _ in range(groups // 2)]
    for number, chunk in enumerate(chunks):
        hidden, give, *turned = chunk_gradient(
            scalars,
            [blocks[k] for k in chunk],
            [others[k] for k in chunk],
            weights,
            groups,
            turn=number == 0,
        )
        weights = list(weights[:2]) + (turned or [weights[2]])
        swapped = flip(give, "rep", 1)
        mine = keep_gradient(scalars, hidden, weights[1], give)
        kinds = [(jnp.bfloat16 if k else jnp.float32, k == wide_size - 1) for k in chunk]
        for k, parts in zip(chunk, join(mine, swapped, kinds)):
            if k == wide_size - 1:
                for index, part in enumerate(parts):
                    far[index].append(straight(part, k, index))
                continue
            part = parts[0]
            if k:
                part = flip(part, "wide", k)
            part = part.astype(jnp.float32)
            near = part if near is None else part + near
    first_core = rep == 0
    keep, give = [], []
    for index in range(groups // 2):
        piece = straight(near[index].astype(jnp.bfloat16), 0, index)
        piece = piece.astype(jnp.float32)
        for part in far[index]:
            piece = piece + part.astype(jnp.float32)
        piece = piece.astype(jnp.bfloat16)
        keep.append(jnp.where(first_core, piece[:height], piece[height:]))
        give.append(jnp.where(first_core, piece[height:], piece[:height]))
    taken = flip(jnp.concatenate(give[::-1], axis=0), "rep", 1)
    pieces = keep + [taken[i * height : (i + 1) * height] for i in range(groups // 2)]
    place = place ^ (rep * (groups - 1))
    bit = 1
    while bit < groups:
        swap = (place & bit) != 0
        pieces = [jnp.where(swap, pieces[k ^ bit], pieces[k]) for k in range(groups)]
        bit *= 2
    return jnp.concatenate(pieces, axis=0)


def shards(hidden_in, grad_out, route_ids, route_weights, gate_proj, up_proj, down_proj):
    wide_size, groups = lax.axis_size("wide"), lax.axis_size("grp")
    experts = gate_proj.shape[0] * wide_size
    fanout = route_ids.shape[1]
    powers = all(n > 1 and n & (n - 1) == 0 for n in (wide_size, groups))
    dense = powers and experts <= 2 * fanout and 2 * experts <= LANES and lax.axis_size("rep") == 2
    path = dense_shards if dense else routed_shards
    return path(
        hidden_in, grad_out, route_ids, route_weights, gate_proj, up_proj, down_proj
    )


def solution(mesh):
    in_specs = (
        P(("wide", "rep"), "grp"),
        P(("wide", "rep"), "grp"),
        P(("wide", "rep"), None),
        P(("wide", "rep"), None),
        P("wide", None, "rep"),
        P("wide", None, "rep"),
        P("wide", "rep", None),
    )
    out_specs = P(("wide", "rep"), "grp")
    return jax.shard_map(
        shards, mesh=mesh, in_specs=in_specs, out_specs=out_specs, check_vma=False
    )
```

```python
import jax
import jax.numpy as jnp
from jax import lax
from jax.experimental import pallas as pl
from jax.experimental.pallas import tpu as pltpu
from jax.sharding import PartitionSpec as P


def expert_back(stacked, gate_mat, up_mat, down_mat):
    inputs = stacked[0]
    scaled = stacked[1]
    pre_gate = jnp.einsum("wecd,edf->wecf", inputs, gate_mat, preferred_element_type=jnp.float32)
    pre_up = jnp.einsum("wecd,edf->wecf", inputs, up_mat, preferred_element_type=jnp.float32)
    back_hidden = jnp.einsum("wecd,efd->wecf", scaled, down_mat, preferred_element_type=jnp.float32)
    gate_sig = jax.nn.sigmoid(pre_gate)
    d_gate = (back_hidden * pre_up * gate_sig * (1.0 + pre_gate * (1.0 - gate_sig))).astype(
        jnp.bfloat16
    )
    d_up = (back_hidden * pre_gate * gate_sig).astype(jnp.bfloat16)
    first_term = jnp.einsum("wecf,edf->wecd", d_gate, gate_mat, preferred_element_type=jnp.float32)
    return first_term + jnp.einsum(
        "wecf,edf->wecd", d_up, up_mat, preferred_element_type=jnp.float32
    )


def slot_ranks(pair_ids, experts):
    pairs = pair_ids.shape[0]
    block = 128
    nblocks = pairs // block
    onehot = (pair_ids[:, None] == jnp.arange(experts, dtype=jnp.int32)[None, :]).astype(
        jnp.bfloat16
    )
    onehot = onehot.reshape(nblocks, block, experts)
    lower = (
        lax.broadcasted_iota(jnp.int32, (block, block), 0)
        > lax.broadcasted_iota(jnp.int32, (block, block), 1)
    ).astype(jnp.bfloat16)
    within = jnp.einsum("ij,bje->bie", lower, onehot, preferred_element_type=jnp.float32)
    totals = jnp.sum(onehot.astype(jnp.float32), axis=1)
    before = jnp.cumsum(totals, axis=0) - totals
    counted = jnp.sum((within + before[:, None, :]) * onehot.astype(jnp.float32), axis=2)
    return counted.reshape(pairs).astype(jnp.int32)


def routed_shards(hidden_in, grad_out, route_ids, route_weights, gate_proj, up_proj, down_proj):
    tok_rows, local_cols = hidden_in.shape
    fanout = route_ids.shape[1]
    wide_size = lax.axis_size("wide")
    groups = lax.axis_size("grp")
    local_experts = gate_proj.shape[0]
    experts = local_experts * wide_size
    capacity = groups * max(1, 3 * tok_rows * fanout // (2 * experts * groups))
    pair_ids = route_ids.reshape(-1)
    slot_rank = slot_ranks(pair_ids, experts)
    position = pair_ids * capacity + slot_rank
    token_ids = jnp.arange(tok_rows * fanout, dtype=jnp.int32) // fanout
    pair_inputs = hidden_in[token_ids]
    pair_scaled = (
        route_weights.reshape(-1)[:, None] * grad_out[token_ids].astype(jnp.float32)
    ).astype(jnp.bfloat16)
    blank_rows = jnp.zeros((experts * capacity, local_cols), jnp.bfloat16)
    outgoing = jnp.stack(
        [blank_rows.at[position].set(pair_inputs), blank_rows.at[position].set(pair_scaled)]
    )
    outgoing = outgoing.reshape(2, wide_size, local_experts, capacity, local_cols)
    received = lax.all_to_all(
        lax.all_to_all(outgoing, "wide", split_axis=1, concat_axis=1, tiled=True),
        "grp",
        split_axis=3,
        concat_axis=4,
        tiled=True,
    )
    full_gate, full_up, full_down = (
        lax.all_gather(gate_proj, "rep", axis=2, tiled=True),
        lax.all_gather(up_proj, "rep", axis=2, tiled=True),
        lax.all_gather(down_proj, "rep", axis=1, tiled=True),
    )
    summed = expert_back(received, full_gate, full_up, full_down)
    returned = lax.all_to_all(
        lax.all_to_all(
            summed.astype(jnp.bfloat16), "wide", split_axis=0, concat_axis=0, tiled=True
        ),
        "grp",
        split_axis=3,
        concat_axis=2,
        tiled=True,
    )
    flat_rows = returned.reshape(experts * capacity, local_cols)
    picked = flat_rows[position].astype(jnp.float32).reshape(tok_rows, fanout, local_cols)
    return jnp.sum(picked, axis=1).astype(jnp.bfloat16)


LANES = 128
VMEM = pl.BlockSpec(memory_space=pltpu.VMEM)
SMEM = pl.BlockSpec(memory_space=pltpu.SMEM)
HBM = pl.BlockSpec(memory_space=pltpu.HBM)


def load_kernel(gate_hbm, up_hbm, down_hbm, after, scalars, both, both_t, down, sems):
    local, _, half = gate_hbm.shape
    halves = (pl.ds(0, half), pl.ds(half, half))
    copies, down_copies = [], []
    for e in range(local):
        for number, source in enumerate((gate_hbm, up_hbm)):
            place = both.at[e, :, halves[number]]
            copies.append(pltpu.make_async_copy(source.at[e], place, sems.at[e, number]))
        place = down.at[pl.ds(e * half, half), :]
        down_copies.append(pltpu.make_async_copy(down_hbm.at[e], place, sems.at[e, 2]))
    for copy in copies + down_copies:
        copy.start()
    for number, copy in enumerate(copies):
        copy.wait()
        e, side = divmod(number, 2)
        both_t[e, side * half : (side + 1) * half] = both[e, :, side * half : (side + 1) * half].T
    for copy in down_copies:
        copy.wait()


def load_weights(gate_proj, up_proj, down_proj, after, scalars):
    local, width, half = gate_proj.shape
    size = 6 * local * width * half
    weights = [pltpu.with_memory_space_constraint(w, pltpu.HBM) for w in (gate_proj, up_proj, down_proj)]
    return pl.pallas_call(
        load_kernel,
        in_specs=[HBM] * 3 + [VMEM, SMEM],
        out_specs=[VMEM] * 3,
        out_shape=[
            jax.ShapeDtypeStruct((local, width, 2 * half), jnp.bfloat16),
            jax.ShapeDtypeStruct((local, 2 * half, width), jnp.bfloat16),
            jax.ShapeDtypeStruct((local * half, width), jnp.bfloat16),
        ],
        scratch_shapes=[pltpu.SemaphoreType.DMA((local, 3))],
        compiler_params=pltpu.CompilerParams(vmem_limit_bytes=8 << 20),
        cost_estimate=pl.CostEstimate(flops=0, bytes_accessed=size, transcendentals=0),
        name="load",
    )(*weights, after, scalars)


def chunk_kernel(groups, count, turn, scalars, *refs):
    place, wide = scalars[0], scalars[1]
    blocks = refs[:count]
    if turn:
        both, both_t, down, hidden_out, give_out, down_t, x_rows, g_rows, total = refs[count:]
    else:
        both, both_t, down_t, hidden_out, give_out, x_rows, g_rows, total = refs[count:]
    local, width, double = both.shape
    half = double // 2
    height = blocks[0].shape[0]
    cols = width // groups
    for number, block in enumerate(blocks):
        rows = slice(number * height, (number + 1) * height)
        for step in range(groups):
            start = pl.multiple_of((place ^ step) * cols, LANES)
            x_rows[rows, pl.ds(start, cols)] = block[:, 2 * step * cols : (2 * step + 1) * cols]
            g_rows[rows, pl.ds(start, cols)] = block[:, (2 * step + 1) * cols : (2 * step + 2) * cols]
    weights = jnp.concatenate([block[:, 2 * width :] for block in blocks], axis=0)
    weights = weights.astype(jnp.float32)
    lane = lax.broadcasted_iota(jnp.int32, weights.shape, 1)
    experts = weights.shape[1] // 2

    for e in range(local):
        named = (lane == wide * local + e) | (lane == wide * local + e + experts)
        route = jnp.sum(jnp.where(named, weights, 0.0), axis=1, keepdims=True)
        if e % 2 == 0:
            pair = slice(e * half, (e + min(2, local - e)) * half)
            if turn:
                down_t[:, pair] = down[pair].T
            back_pair = jnp.dot(
                g_rows[...],
                down_t[:, pair],
                preferred_element_type=jnp.float32,
            )
        pre = jnp.dot(x_rows[...], both[e], preferred_element_type=jnp.float32)
        back = route * back_pair[:, (e % 2) * half : (e % 2 + 1) * half]
        pre_gate, pre_up = pre[:, :half], pre[:, half:]
        sig = 1.0 / (1.0 + jnp.exp(-pre_gate))
        d_gate = back * pre_up * sig * (1.0 + pre_gate * (1.0 - sig))
        d_up = back * pre_gate * sig
        hidden = jnp.concatenate([d_gate, d_up], axis=1).astype(jnp.bfloat16)
        hidden_out[e] = hidden
        add_places(scalars, 1 - scalars[2], hidden, both_t, e, total)
    put_places(scalars, total, give_out)


def even(index):
    return 2 * index + bin(index).count("1") % 2


def add_places(scalars, core, hidden, both_t, e, total):
    cols = total.shape[2]
    for index in range(total.shape[0]):
        start = (scalars[0] ^ core ^ even(index)) * cols
        columns = pl.ds(pl.multiple_of(start, LANES), cols)
        term = jnp.dot(hidden, both_t[e, :, columns], preferred_element_type=jnp.float32)
        if e == 0:
            total[index] = term
        else:
            total[index] += term


def put_places(scalars, total, out):
    slots, _, double, _ = out.shape
    height = double // 2
    for index in range(total.shape[0]):
        for slot in range(slots):
            for rep in range(2):
                first = pl.multiple_of(((scalars[2] ^ rep) * slots + slot) * height, height)
                part = total[index, pl.ds(first, height), :]
                out[slot, index, rep * height : (rep + 1) * height, :] = part.astype(out.dtype)


def keep_kernel(scalars, hidden, both_t, keep_out, total):
    for e in range(hidden.shape[0]):
        add_places(scalars, scalars[2], hidden[e], both_t, e, total)
    put_places(scalars, total, keep_out)


def keep_gradient(scalars, hidden, both_t, give):
    local, rows, double = hidden.shape
    _, places, _, cols = give.shape
    return pl.pallas_call(
        keep_kernel,
        in_specs=[SMEM] + [VMEM] * 2,
        out_specs=VMEM,
        out_shape=jax.ShapeDtypeStruct(give.shape, jnp.float32),
        scratch_shapes=[pltpu.VMEM((places, rows, cols), jnp.float32)],
        compiler_params=pltpu.CompilerParams(vmem_limit_bytes=16 * rows * places * cols),
        cost_estimate=pl.CostEstimate(
            flops=2 * rows * double * places * cols * local,
            bytes_accessed=2 * local * rows * double,
            transcendentals=0,
        ),
        name="keep",
    )(scalars, hidden, both_t)


def chunk_gradient(scalars, mine, other, weights, groups, turn):
    local, width, double = weights[0].shape
    slots, height = len(mine), mine[0].shape[0]
    rows = 2 * slots * height
    shape = (slots, groups // 2, 2 * height, width // groups)
    return pl.pallas_call(
        lambda *refs: chunk_kernel(groups, 2 * slots, turn, *refs),
        in_specs=[SMEM] + [VMEM] * (2 * slots + 3),
        out_specs=[VMEM] * (3 if turn else 2),
        out_shape=[
            jax.ShapeDtypeStruct((local, rows, double), jnp.bfloat16),
            jax.ShapeDtypeStruct(shape, jnp.bfloat16),
        ]
        + [jax.ShapeDtypeStruct(weights[2].shape[::-1], jnp.bfloat16)] * turn,
        scratch_shapes=[
            pltpu.VMEM((rows, width), jnp.bfloat16),
            pltpu.VMEM((rows, width), jnp.bfloat16),
            pltpu.VMEM((groups // 2, rows, width // groups), jnp.float32),
        ],
        compiler_params=pltpu.CompilerParams(vmem_limit_bytes=16 * rows * width),
        cost_estimate=pl.CostEstimate(
            flops=10 * 256 * width * (double // 2) * local // 2,
            bytes_accessed=4 * rows * width,
            transcendentals=rows * (double // 2) * local,
        ),
        name="chunk",
    )(scalars, *mine, *other, *weights)


def join_kernel(kinds, mine, swapped, *outs):
    for slot, (_, cut) in enumerate(kinds):
        part = mine[slot] + swapped[slot].astype(jnp.float32)
        for index in range(part.shape[0] if cut else 1):
            out, outs = outs[0], outs[1:]
            out[...] = (part[index] if cut else part).astype(out.dtype)


def join(mine, swapped, kinds):
    shape = mine.shape[1:]
    shapes = []
    for kind, cut in kinds:
        shapes += [jax.ShapeDtypeStruct(shape[1:], kind)] * shape[0] if cut else [jax.ShapeDtypeStruct(shape, kind)]
    outs = pl.pallas_call(
        lambda *refs: join_kernel(kinds, *refs),
        in_specs=[VMEM] * 2,
        out_specs=[VMEM] * len(shapes),
        out_shape=shapes,
        compiler_params=pltpu.CompilerParams(vmem_limit_bytes=1 << 20),
        name="join",
    )(mine, swapped)
    slots = []
    for _, cut in kinds:
        number = shape[0] if cut else 1
        slots.append(outs[:number])
        outs = outs[number:]
    return slots


def flip(array, axis, step):
    size = lax.axis_size(axis)
    return lax.ppermute(array, axis, [(i, i ^ step) for i in range(size)])


def straight(array, wide_step, index):
    wide_size, groups = lax.axis_size("wide"), lax.axis_size("grp")
    pairs = []
    for w in range(wide_size):
        for g in range(groups):
            for r in range(2):
                target = (w ^ wide_step) * groups + (g ^ r ^ even(index))
                pairs.append(((w * groups + g) * 2 + r, target * 2 + r))
    return lax.ppermute(array, ("wide", "grp", "rep"), pairs)


def route_table(route_ids, route_weights, experts):
    chosen = route_ids[:, :, None] == jnp.arange(experts, dtype=jnp.int32)[None, None, :]
    return jnp.sum(jnp.where(chosen, route_weights[:, :, None], 0.0), axis=1)


def gathered(block, far_block, axis):
    size = lax.axis_size(axis)
    parts = {0: block, size // 2: far_block}
    step = size // 4
    while step:
        for k in sorted(parts):
            parts[k | step] = flip(parts[k], axis, step)
        step //= 2
    return [parts[k] for k in range(size)]


def dense_shards(hidden_in, grad_out, route_ids, route_weights, gate_proj, up_proj, down_proj):
    tok_rows, _ = hidden_in.shape
    wide_size = lax.axis_size("wide")
    groups = lax.axis_size("grp")
    local = gate_proj.shape[0]
    height = tok_rows // groups
    place = lax.axis_index("grp").astype(jnp.int32)
    wide = lax.axis_index("wide").astype(jnp.int32)
    rep = lax.axis_index("rep").astype(jnp.int32)
    scalars = jnp.stack([place, wide, rep])

    pieces = []
    for step in range(groups):
        first = (place ^ step) * height
        piece = jnp.concatenate(
            [lax.dynamic_slice_in_dim(a, first, height, 0) for a in (hidden_in, grad_out)], axis=1
        )
        pieces.append(piece if step == 0 else flip(piece, "grp", step))
    half_way = wide_size // 2
    early = flip(pieces[0], "wide", half_way)
    ids = lax.dynamic_slice_in_dim(route_ids, place * height, height, 0)
    route = lax.dynamic_slice_in_dim(route_weights, place * height, height, 0)
    table = route_table(ids, route, local * wide_size)
    table = jnp.pad(table, ((0, 0), (0, LANES // 2 - table.shape[1])))
    high = table.astype(jnp.bfloat16)
    low = (table - high.astype(jnp.float32)).astype(jnp.bfloat16)
    rest = jnp.concatenate(pieces[1:] + [high, low], axis=1)
    far_block = jnp.concatenate([early, flip(rest, "wide", half_way)], axis=1)
    block = jnp.concatenate([pieces[0], rest], axis=1)
    weights = load_weights(gate_proj, up_proj, down_proj, block, scalars)
    blocks = gathered(block, far_block, "wide")
    chunks = [list(range(first, wide_size, 2))[::-1] for first in (0, 1)]
    others = []
    for k in range(wide_size):
        others.append(flip(blocks[k], "rep", 1))
    near, far = None, [[] for _ in range(groups // 2)]
    for number, chunk in enumerate(chunks):
        hidden, give, *turned = chunk_gradient(
            scalars,
            [blocks[k] for k in chunk],
            [others[k] for k in chunk],
            weights,
            groups,
            turn=number == 0,
        )
        weights = list(weights[:2]) + (turned or [weights[2]])
        swapped = flip(give, "rep", 1)
        mine = keep_gradient(scalars, hidden, weights[1], give)
        kinds = [(jnp.bfloat16 if k else jnp.float32, k == wide_size - 1) for k in chunk]
        for k, parts in zip(chunk, join(mine, swapped, kinds)):
            if k == wide_size - 1:
                for index, part in enumerate(parts):
                    far[index].append(straight(part, k, index))
                continue
            part = parts[0]
            if k:
                part = flip(part, "wide", k)
            part = part.astype(jnp.float32)
            near = part if near is None else part + near
    first_core = rep == 0
    keep, give = [], []
    for index in range(groups // 2):
        piece = straight(near[index].astype(jnp.bfloat16), 0, index)
        piece = piece.astype(jnp.float32)
        for part in far[index]:
            piece = piece + part.astype(jnp.float32)
        piece = piece.astype(jnp.bfloat16)
        keep.append(jnp.where(first_core, piece[:height], piece[height:]))
        give.append(jnp.where(first_core, piece[height:], piece[:height]))
    taken = flip(jnp.concatenate(give, axis=0), "rep", 1)
    pieces = [None] * groups
    for index in range(groups // 2):
        pieces[even(index)] = keep[index]
        pieces[even(index) ^ 1] = taken[index * height : (index + 1) * height]
    place = place ^ rep
    bit = 1
    while bit < groups:
        swap = (place & bit) != 0
        pieces = [jnp.where(swap, pieces[k ^ bit], pieces[k]) for k in range(groups)]
        bit *= 2
    return jnp.concatenate(pieces, axis=0)


def shards(hidden_in, grad_out, route_ids, route_weights, gate_proj, up_proj, down_proj):
    wide_size, groups = lax.axis_size("wide"), lax.axis_size("grp")
    experts = gate_proj.shape[0] * wide_size
    fanout = route_ids.shape[1]
    powers = all(n > 1 and n & (n - 1) == 0 for n in (wide_size, groups))
    dense = powers and experts <= 2 * fanout and 2 * experts <= LANES and lax.axis_size("rep") == 2
    path = dense_shards if dense else routed_shards
    return path(
        hidden_in, grad_out, route_ids, route_weights, gate_proj, up_proj, down_proj
    )


def solution(mesh):
    in_specs = (
        P(("wide", "rep"), "grp"),
        P(("wide", "rep"), "grp"),
        P(("wide", "rep"), None),
        P(("wide", "rep"), None),
        P("wide", None, "rep"),
        P("wide", None, "rep"),
        P("wide", "rep", None),
    )
    out_specs = P(("wide", "rep"), "grp")
    return jax.shard_map(
        shards, mesh=mesh, in_specs=in_specs, out_specs=out_specs, check_vma=False
    )
```
